32 devices in a mesh: half: 2 (over y), row: 4 (over z), col: 4 (over x, core).
Axes of the slice: x: 2, y: 2, z: 4, core: 2. Of those that a mesh axis runs over, the one named last changes fastest.
Arguments:
- front_init: float32 [10240, 10240], P(('half', 'row'), 'col'), may hold values from -2 to 8, as said below
- child_update: float32 [2, 8192, 8192], P('half', 'row', 'col'), may hold values from -2 to 8, as said below
- child_map: int32 [2, 8192], replicated, may hold values from 0 to 10239, as said below
Outputs:
- factor_front: float32 [10240, 10240], P(('half', 'row'), 'col')
The draws below stay inside these ranges and needn't reach their ends.
Inputs may be any that keep to these rules, and one draw needn't show every extreme that they name: `child_map`: each child's entries are distinct. Each aligned block of 128 child indices maps onto one whole block of 128 front indices; write b(j) for the front block of child block j. For every r and q below 4, exactly 4 child blocks j with j % 4 == r have b(j) % 4 == q, and these share one value of b(j) % 8. Symmetric in natural order, and front_init minus the identity is positive semidefinite. `child_update`: each child's matrix is symmetric positive semidefinite.
All inputs are finite; a program needn't handle non-finite values.
Results may differ from the reference program's by a relative error of at most 0.0001.
Values sent between devices are 32-bit elements; how exact they have to be, the bound alone decides.
A program may use at most 256 MiB of HBM per device.

```python
import jax
import jax.numpy as jnp
from jax import lax

F = 10240
UC = 8192
BLOCK_EDGE = 128
PANELS = 2
DEVICE_GRID = 4
HALVES = 2
ROW_GROUPS = 8
GROUP_ROWS = 10
FRONT_COLUMNS = 20
CRB = 16
CB = 64
CAP = 4
PANEL = 256


def rough_matrix(key, rows, cols):
    return jnp.clip(jax.random.normal(key, (rows, cols), jnp.float32), -5.0, 5.0)


def gram_matrix(key, order, rank_width):
    subkeys = jax.random.split(key, 1)
    factor_rows = rough_matrix(subkeys[0], order, rank_width)
    product = jnp.dot(factor_rows, factor_rows.T, precision=lax.Precision.HIGHEST) / rank_width
    return (product + product.T) * 0.5


def draw_front_init(key, part):
    gram = gram_matrix(jax.random.fold_in(key, 301), F, F // 10)
    natural_order = gram + jnp.eye(F, dtype=jnp.float32)
    reshaped_front = natural_order.reshape(GROUP_ROWS, ROW_GROUPS, BLOCK_EDGE, FRONT_COLUMNS, DEVICE_GRID, BLOCK_EDGE)
    return reshaped_front.transpose(1, 0, 2, 4, 3, 5).reshape(F, F)


def draw_child_update(key, part):
    results = []
    for which_child in range(2):
        results.append(gram_matrix(jax.random.fold_in(key, 401 + which_child), UC, UC // 8))
    return jnp.stack(results)


def one_child_map(key):
    subkeys = jax.random.split(key, 4)
    per_half = GROUP_ROWS // CAP
    slot_total = HALVES * per_half
    chosen = jax.vmap(lambda subkey: jax.random.permutation(subkey, slot_total)[:DEVICE_GRID])(jax.random.split(subkeys[0], DEVICE_GRID))
    within = jax.vmap(lambda subkey: jax.random.permutation(subkey, GROUP_ROWS))(jax.random.split(subkeys[1], DEVICE_GRID * HALVES))
    within = within.reshape(DEVICE_GRID, HALVES, GROUP_ROWS)
    half_pick = chosen // per_half
    offset = chosen % per_half
    picked_rows = within[jnp.arange(DEVICE_GRID)[:, None], half_pick]
    positions = offset[:, :, None] * CAP + jnp.arange(CAP)[None, None, :]
    block_rows = jnp.take_along_axis(picked_rows, positions, axis=2)
    front_block = (half_pick * DEVICE_GRID + jnp.arange(DEVICE_GRID)[:, None])[:, :, None] + ROW_GROUPS * block_rows
    by_row = front_block.transpose(1, 0, 2).reshape(DEVICE_GRID, DEVICE_GRID * CAP)
    local_order = jax.vmap(lambda subkey: jax.random.permutation(subkey, DEVICE_GRID * CAP))(jax.random.split(subkeys[2], DEVICE_GRID))
    placed = jnp.zeros((DEVICE_GRID, DEVICE_GRID * CAP), jnp.int32).at[jnp.arange(DEVICE_GRID)[:, None], local_order].set(by_row.astype(jnp.int32))
    block_map = placed.T.reshape(CB)
    inner_perm = jax.vmap(lambda subkey: jax.random.permutation(subkey, BLOCK_EDGE))(jax.random.split(subkeys[3], CB))
    return (block_map[:, None] * BLOCK_EDGE + inner_perm).reshape(UC).astype(jnp.int32)


def draw_child_map(key, part):
    return jnp.stack([one_child_map(jax.random.fold_in(key, 501 + which_child)) for which_child in range(2)])


def setup_inputs(seed: int = 0) -> dict:
    keys = jax.random.split(jax.random.key(seed), 4)
    return {
        "front_init": draw_front_init(jax.random.fold_in(keys[3], 71), 0),
        "child_update": draw_child_update(jax.random.fold_in(keys[3], 71), 0),
        "child_map": draw_child_map(jax.random.fold_in(keys[3], 71), 0),
    }


def front_natural(stored_layout):
    reshaped_front = stored_layout.reshape(ROW_GROUPS, GROUP_ROWS, BLOCK_EDGE, DEVICE_GRID, FRONT_COLUMNS, BLOCK_EDGE)
    return reshaped_front.transpose(1, 0, 2, 4, 3, 5).reshape(F, F)

def front_stored(natural_order):
    reshaped_front = natural_order.reshape(GROUP_ROWS, ROW_GROUPS, BLOCK_EDGE, FRONT_COLUMNS, DEVICE_GRID, BLOCK_EDGE)
    return reshaped_front.transpose(1, 0, 2, 4, 3, 5).reshape(F, F)

def child_natural(stored_layout):
    reshaped_front = stored_layout.reshape(DEVICE_GRID, CRB, BLOCK_EDGE, DEVICE_GRID, CRB, BLOCK_EDGE)
    return reshaped_front.transpose(1, 0, 2, 4, 3, 5).reshape(UC, UC)

def reference(front_init, child_update, child_map):
    front_local = front_natural(front_init)
    for which_child in range(2):
        update = child_natural(child_update[which_child])
        targets = child_map[which_child]
        spread = jnp.zeros((UC, F), jnp.float32).at[:, targets].set(update)
        front_local = front_local.at[targets].add(spread)
    identity = jnp.eye(PANEL, dtype=jnp.float32)
    row_ids = jnp.arange(F)
    for panel_index in range(PANELS):
        panel_start = panel_index * PANEL
        panel_end = panel_start + PANEL
        factor = jnp.linalg.cholesky(front_local[panel_start:panel_end, panel_start:panel_end])
        inverse = lax.linalg.triangular_solve(factor, identity, left_side=True, lower=True)
        lower_rows = jnp.dot(front_local[:, panel_start:panel_end], inverse.T, precision=lax.Precision.HIGHEST)
        lower_rows = jnp.where((row_ids >= panel_start)[:, None], lower_rows, 0.0)
        tail_rows = lower_rows[panel_end:]
        update = jnp.dot(tail_rows, tail_rows.T, precision=lax.Precision.HIGHEST)
        front_local = front_local.at[panel_end:, panel_end:].set(front_local[panel_end:, panel_end:] - update)
        front_local = front_local.at[:, panel_start:panel_end].set(lower_rows)
        front_local = front_local.at[panel_start:panel_end, panel_end:].set(0.0)
    return front_stored(front_local)
```

```python
import functools

import jax
import jax.numpy as jnp
from jax import lax
from jax.experimental import pallas as pl
from jax.experimental.pallas import tpu as pltpu
from jax.sharding import PartitionSpec as P

BE = 128
PANEL = 256
WIDE = 512
HIGHEST = lax.Precision.HIGHEST
F32 = jnp.float32
BF16 = jnp.bfloat16
NT = (((1,), (1,)), ((), ()))


def absdiff(a, b):
    return jnp.maximum(a - b, b - a)


def use_direct(a, b, x, y):
    direct = 2 * absdiff(a, x) + absdiff(b // 2, y // 2)
    swapped = 2 * absdiff(b, x) + absdiff(a // 2, y // 2)
    return direct <= swapped


def pack_kernel(grid_size, slots, row_order, col_order, src, dst):
    for y in range(grid_size):
        for k in range(slots):
            at = pl.multiple_of(col_order[y * slots + k] * BE, BE)
            dst[0, y, 0, k] = src[:, pl.ds(at, BE)]


def pack(child, row_order, col_order, grid_size, slots):
    rows, cols = child.shape
    return pl.pallas_call(
        functools.partial(pack_kernel, grid_size, slots),
        grid_spec=pltpu.PrefetchScalarGridSpec(
            num_scalar_prefetch=2,
            grid=(grid_size * slots,),
            in_specs=[pl.BlockSpec((BE, cols), lambda n, ro, co: (ro[n], 0))],
            out_specs=pl.BlockSpec(
                (1, grid_size, 1, slots, BE, BE),
                lambda n, ro, co: (n // slots, 0, n % slots, 0, 0, 0),
            ),
        ),
        out_shape=jax.ShapeDtypeStruct((grid_size, grid_size, slots, slots, BE, BE), F32),
    )(row_order, col_order, child)


def exchange_kernel(
    grid_size, src, dst, relay, send_direct, send_swap, recv, local,
    relay_recv, relay_send,
):
    r = lax.axis_index("row")
    s = lax.axis_index("col")
    half = lax.axis_index("half")
    g = grid_size

    def peer(k):
        return (r + k // g) % g, (s + k % g) % g

    barrier = pltpu.get_barrier_semaphore()

    def greet(k, carry):
        x, y = peer(k)
        pl.semaphore_signal(
            barrier, inc=1, device_id=(half, x, y), device_id_type=pl.DeviceIdType.MESH
        )
        return carry

    lax.fori_loop(1, g * g, greet, 0)
    pl.semaphore_wait(barrier, g * g - 1)

    own = pltpu.make_async_copy(src.at[r, s], dst.at[r, s], local.at[0])
    own_swap = pltpu.make_async_copy(src.at[s, r], dst.at[s, r], local.at[1])
    own.start()

    @pl.when(r != s)
    def _():
        own_swap.start()

    def turns(x, y):
        return jnp.logical_and(x != r, y // 2 != s // 2)

    def first_hop(kind, k, x, y):
        source = src.at[y, x] if kind else src.at[x, y]
        return pltpu.make_async_remote_copy(
            src_ref=source,
            dst_ref=relay.at[s, x, kind],
            send_sem=(send_swap if kind else send_direct).at[k],
            recv_sem=relay_recv.at[(s * g + x) * 2 + kind],
            device_id=(half, r, y),
            device_id_type=pl.DeviceIdType.MESH,
        )

    def second_hop(kind, b, x):
        at = (b * g + x) * 2 + kind
        target, slot = (dst.at[b, r], b * g + r) if kind else (dst.at[r, b], r * g + b)
        return pltpu.make_async_remote_copy(
            src_ref=relay.at[b, x, kind],
            dst_ref=target,
            send_sem=relay_send.at[at],
            recv_sem=recv.at[slot],
            device_id=(half, x, s),
            device_id_type=pl.DeviceIdType.MESH,
        )

    def whole_way(kind, k, x, y):
        source, target, slot = (
            (src.at[y, x], dst.at[s, r], s * g + r)
            if kind
            else (src.at[x, y], dst.at[r, s], r * g + s)
        )
        return pltpu.make_async_remote_copy(
            src_ref=source,
            dst_ref=target,
            send_sem=(send_swap if kind else send_direct).at[k],
            recv_sem=recv.at[slot],
            device_id=(half, x, y),
            device_id_type=pl.DeviceIdType.MESH,
        )

    def wanted(kind, a, b, x, y):
        if kind:
            return jnp.logical_not(use_direct(b, a, x, y))
        return use_direct(a, b, x, y)

    def send_turning(k, carry):
        x, y = peer(k)
        for kind in range(2):

            @pl.when(jnp.logical_and(turns(x, y), wanted(kind, r, s, x, y)))
            def _():
                first_hop(kind, k, x, y).start()

        return carry

    lax.fori_loop(1, g * g, send_turning, 0)

    def send_straight(k, carry):
        x, y = peer(k)
        for kind in range(2):

            @pl.when(
                jnp.logical_and(
                    jnp.logical_not(turns(x, y)), wanted(kind, r, s, x, y)
                )
            )
            def _():
                whole_way(kind, k, x, y).start()

        return carry

    lax.fori_loop(1, g * g, send_straight, 0)

    def relayed(k):
        x = (r + k // g) % g
        b = (s + g - k % g) % g
        return b, x

    def pass_on(k, carry):
        b, x = relayed(k)
        for kind in range(2):

            @pl.when(
                jnp.logical_and(
                    jnp.logical_and(x != r, b // 2 != s // 2), wanted(kind, r, b, x, s)
                )
            )
            def _():
                pltpu.make_async_remote_copy(
                    src_ref=src.at[x, b],
                    dst_ref=relay.at[b, x, kind],
                    send_sem=send_direct.at[0],
                    recv_sem=relay_recv.at[(b * g + x) * 2 + kind],
                    device_id=(half, r, (s + 1) % g),
                    device_id_type=pl.DeviceIdType.MESH,
                ).wait_recv()
                second_hop(kind, b, x).start()

        return carry

    lax.fori_loop(1, g * g, pass_on, 0)

    def passed_on(k, carry):
        b, x = relayed(k)
        for kind in range(2):

            @pl.when(
                jnp.logical_and(
                    jnp.logical_and(x != r, b // 2 != s // 2), wanted(kind, r, b, x, s)
                )
            )
            def _():
                second_hop(kind, b, x).wait_send()

        return carry

    lax.fori_loop(1, g * g, passed_on, 0)

    def sent(k, carry):
        x, y = peer(k)
        for kind in range(2):

            @pl.when(wanted(kind, r, s, x, y))
            def _():
                whole_way(kind, k, x, y).wait_send()

        return carry

    lax.fori_loop(1, g * g, sent, 0)

    def arrived(k, carry):
        a = k // g
        b = k % g
        mine = jnp.logical_or(
            jnp.logical_and(a == r, b == s), jnp.logical_and(a == s, b == r)
        )

        @pl.when(jnp.logical_not(mine))
        def _():
            pltpu.make_async_remote_copy(
                src_ref=src.at[a, b],
                dst_ref=dst.at[a, b],
                send_sem=send_direct.at[0],
                recv_sem=recv.at[k],
                device_id=(half, (r + 1) % g, s),
                device_id_type=pl.DeviceIdType.MESH,
            ).wait_recv()

        return carry

    lax.fori_loop(0, g * g, arrived, 0)
    own.wait()

    @pl.when(r != s)
    def _():
        own_swap.wait()


def exchange(packed, grid_size):
    n = grid_size * grid_size
    return pl.pallas_call(
        functools.partial(exchange_kernel, grid_size),
        out_shape=[
            jax.ShapeDtypeStruct(packed.shape, F32),
            jax.ShapeDtypeStruct((grid_size, grid_size, 2) + packed.shape[2:], F32),
        ],
        in_specs=[pl.BlockSpec(memory_space=pl.ANY)],
        out_specs=[pl.BlockSpec(memory_space=pl.ANY)] * 2,
        scratch_shapes=[
            pltpu.SemaphoreType.DMA((n,)),
            pltpu.SemaphoreType.DMA((n,)),
            pltpu.SemaphoreType.DMA((n,)),
            pltpu.SemaphoreType.DMA((2,)),
            pltpu.SemaphoreType.DMA((2 * n,)),
            pltpu.SemaphoreType.DMA((2 * n,)),
        ],
        compiler_params=pltpu.CompilerParams(collective_id=0, has_side_effects=True),
    )(packed)[0]


def split(x):
    high = x.astype(BF16)
    return high, (x - high.astype(F32)).astype(BF16)


def place_kernel(
    grid_size, slots, steps, finish, chunk_at, t_at, u_at, swapped, valid, place_of,
    front, chunk, row_perm, col_perm, lower_col, out, acc, mid, sem,
):
    n = pl.program_id(0)
    a = n // grid_size
    s = n % grid_size

    @pl.when(n == 0)
    def _():
        load = pltpu.make_async_copy(front, acc, sem)
        load.start()
        load.wait()

    @pl.when(valid[a] == 1)
    def _():
        @pl.when(swapped[n] == 1)
        def _():
            for i in range(slots):
                high, low = split(
                    jnp.concatenate([chunk[0, k, i] for k in range(slots)], axis=0)
                )
                perm = row_perm[0, i]
                rows = slice(i * BE, (i + 1) * BE)
                for part, x in enumerate((high, low)):
                    moved = lax.dot_general(perm, x, NT, preferred_element_type=F32)
                    for k in range(slots):
                        at = (2 * k + part) * BE
                        mid[rows, at : at + BE] = moved[:, k * BE : (k + 1) * BE].astype(BF16)

        @pl.when(swapped[n] == 0)
        def _():
            for i in range(slots):
                high, low = split(
                    jnp.concatenate([chunk[0, i, k] for k in range(slots)], axis=1)
                )
                perm = row_perm[0, i]
                rows = slice(i * BE, (i + 1) * BE)
                for part, x in enumerate((high, low)):
                    moved = jnp.dot(perm, x, preferred_element_type=F32)
                    for k in range(slots):
                        at = (2 * k + part) * BE
                        mid[rows, at : at + BE] = moved[:, k * BE : (k + 1) * BE].astype(BF16)

        for k in range(slots):
            u = pl.multiple_of(u_at[s * slots + k] * BE, BE)
            perm2 = jnp.concatenate([col_perm[0, k], col_perm[0, k]], axis=1)
            moved = lax.dot_general(
                mid[:, 2 * k * BE : 2 * (k + 1) * BE], perm2, NT, preferred_element_type=F32
            )
            for i in range(slots):
                t = pl.multiple_of(t_at[a * slots + i] * BE, BE)
                acc[pl.ds(t, BE), pl.ds(u, BE)] += moved[i * BE : (i + 1) * BE]

    @pl.when(n == steps - 1)
    def _():
        if finish:
            @pl.when(place_of[0] < WIDE // BE)
            def _():
                acc[:BE, :] = jnp.zeros((BE, acc.shape[1]), F32)

            @pl.when(place_of[1] < WIDE // BE)
            def _():
                acc[:, :BE] = lower_col[...]

        store = pltpu.make_async_copy(acc, out, sem)
        store.start()
        store.wait()


def place(front, chunks, chunk_at, t, place_of, lower_col, grid_size, finish):
    slots = t["row_perm"].shape[1]
    steps = t["row_perm"].shape[0] * grid_size
    return pl.pallas_call(
        functools.partial(place_kernel, grid_size, slots, steps, finish),
        grid_spec=pltpu.PrefetchScalarGridSpec(
            num_scalar_prefetch=6,
            grid=(steps,),
            in_specs=[
                pl.BlockSpec(memory_space=pl.ANY),
                pl.BlockSpec((1, slots, slots, BE, BE), lambda n, ca, *_: (ca[n], 0, 0, 0, 0)),
                pl.BlockSpec((1, slots, BE, BE), lambda n, *_: (n // grid_size, 0, 0, 0)),
                pl.BlockSpec((1, slots, BE, BE), lambda n, *_: (n % grid_size, 0, 0, 0)),
                pl.BlockSpec((front.shape[0], BE), lambda n, *_: (0, 0)),
            ],
            out_specs=pl.BlockSpec(memory_space=pl.ANY),
            scratch_shapes=[
                pltpu.VMEM(front.shape, F32),
                pltpu.VMEM((slots * BE, 2 * slots * BE), BF16),
                pltpu.SemaphoreType.DMA,
            ],
        ),
        out_shape=jax.ShapeDtypeStruct(front.shape, F32),
        compiler_params=pltpu.CompilerParams(vmem_limit_bytes=40 * 1024 * 1024),
        cost_estimate=pl.CostEstimate(
            flops=4_000_000_000, bytes_accessed=36_000_000, transcendentals=0
        ),
    )(
        chunk_at, t["t_at"], t["u_at"], t["swapped"], t["valid"], place_of,
        front, chunks, t["row_perm"], t["col_perm"], lower_col,
    )


def update_kernel(front, lrow, lcol, out, col_high, col_low):
    @pl.when(pl.program_id(0) == 0)
    def _():
        high, low = split(lcol[...])
        col_high[...] = high
        col_low[...] = low

    high, low = split(lrow[...])
    width = out.shape[1]
    step = WIDE if width % WIDE == 0 else 2 * BE
    for at in range(0, width, step):
        cols = slice(at, at + step)
        ch = col_high[cols, :]
        total = lax.dot_general(high, ch, NT, preferred_element_type=F32)
        total += lax.dot_general(low, ch, NT, preferred_element_type=F32)
        total += lax.dot_general(high, col_low[cols, :], NT, preferred_element_type=F32)
        out[:, cols] = front[:, cols] - total


def update(front, lrow, lcol):
    rows, cols = front.shape
    tall = 2 * BE if rows % (2 * BE) == 0 else BE
    return pl.pallas_call(
        update_kernel,
        grid=(rows // tall,),
        in_specs=[
            pl.BlockSpec((tall, cols), lambda t: (t, 0)),
            pl.BlockSpec((tall, WIDE), lambda t: (t, 0)),
            pl.BlockSpec((cols, WIDE), lambda t: (0, 0)),
        ],
        out_specs=pl.BlockSpec((tall, cols), lambda t: (t, 0)),
        scratch_shapes=[pltpu.VMEM((cols, WIDE), BF16), pltpu.VMEM((cols, WIDE), BF16)],
        out_shape=jax.ShapeDtypeStruct(front.shape, F32),
        compiler_params=pltpu.CompilerParams(vmem_limit_bytes=48 * 1024 * 1024),
        cost_estimate=pl.CostEstimate(
            flops=10_000_000_000, bytes_accessed=34_000_000, transcendentals=0
        ),
    )(front, lrow, lcol)


def factor_block(work, start):
    sub = lax.broadcasted_iota(jnp.int32, (BE, 1), 0)
    lane = lax.broadcasted_iota(jnp.int32, (BE, BE), 1)

    def eliminate(j, carry):
        row = work[pl.ds(j, 1), :]
        whole = work[...]
        column = jnp.sum(jnp.where(lane == j, whole[:, :BE], 0.0), axis=1, keepdims=True)
        pivot = jnp.sum(jnp.where(sub == j, column, 0.0), axis=0, keepdims=True)
        root = lax.rsqrt(pivot)
        root = root * (1.5 - 0.5 * pivot * root * root)
        by = jnp.where(sub > j, column * (root * root), jnp.where(sub == j, 1.0 - root, 0.0))
        work[...] = whole - by * row
        return carry

    lax.fori_loop(start, start + BE, eliminate, 0)


def highest(a, b, dims=(((1,), (0,)), ((), ()))):
    return lax.dot_general(a, b, dims, precision=HIGHEST, preferred_element_type=F32)


def invert_kernel(diagonal, inverse, schur, work):
    row_at = lax.broadcasted_iota(jnp.int32, (WIDE, WIDE), 0)
    col_at = lax.broadcasted_iota(jnp.int32, (WIDE, WIDE), 1)
    eye = jnp.where(row_at == col_at, 1.0, 0.0).astype(F32)
    schur[...] = diagonal[...]
    inverse[...] = eye
    for k in range(WIDE // BE):
        rows = slice(k * BE, (k + 1) * BE)
        rest = slice((k + 1) * BE, WIDE)
        work[:, :BE] = schur[rows, rows]
        work[:, BE:] = eye[:BE, :BE]
        factor_block(work, 0)
        small = work[:, BE:]
        mine = highest(small, inverse[rows, :])
        inverse[rows, :] = mine
        if k + 1 < WIDE // BE:
            below = highest(schur[rest, rows], small, NT)
            schur[rest, rest] = schur[rest, rest] - highest(below, below, NT)
            inverse[rest, :] = inverse[rest, :] - highest(below, mine)


def invert(diagonal):
    return pl.pallas_call(
        invert_kernel,
        in_specs=[pl.BlockSpec(memory_space=pltpu.VMEM)],
        out_specs=pl.BlockSpec(memory_space=pltpu.VMEM),
        scratch_shapes=[pltpu.VMEM((WIDE, WIDE), F32), pltpu.VMEM((BE, 2 * BE), F32)],
        out_shape=jax.ShapeDtypeStruct((WIDE, WIDE), F32),
        compiler_params=pltpu.CompilerParams(vmem_limit_bytes=24 * 1024 * 1024),
        cost_estimate=pl.CostEstimate(
            flops=40_000_000_000, bytes_accessed=4_000_000, transcendentals=0
        ),
    )(diagonal)


def pick(hits, count):
    ids = jnp.arange(hits.shape[-1])
    earlier = jnp.logical_and(hits[..., None, :], ids[None, :] < ids[:, None])
    rank = jnp.sum(earlier.astype(jnp.int32), axis=-1)
    chosen = jnp.logical_and(hits[..., None, :], rank[..., None, :] == jnp.arange(count)[:, None])
    return chosen, jnp.sum(jnp.where(chosen, ids, 0), axis=-1)


def all_tables(child_map, grid_size, group_count, my_row, my_col, my_half, cap, slots):
    g, n = grid_size, slots
    halves = child_map.shape[0]
    maps = child_map.reshape(halves, n * g, g, BE).transpose(0, 2, 1, 3)
    block = maps[..., 0] // BE
    inner = maps % BE
    target = block % g
    before = jnp.logical_and(
        target[..., None, :] == target[..., :, None], block[..., None, :] < block[..., :, None]
    )
    at = target * n + jnp.sum(before.astype(jnp.int32), axis=-1)
    hot = at[..., None, :] == jnp.arange(n * g)[:, None]
    order = jnp.sum(jnp.where(hot, jnp.arange(n * g), 0), axis=-1)
    blocks = jnp.sum(jnp.where(hot, block[..., None, :], 0), axis=-1)

    def of_target(x, which):
        return lax.dynamic_slice_in_dim(x, which * n, n, axis=2)

    inner_of = jnp.sum(
        jnp.where(hot[..., None], inner[:, :, None], 0), axis=3
    )
    row_blocks = of_target(blocks, my_row)
    col_blocks = of_target(blocks, my_col)
    half_of = row_blocks[..., 0] % group_count // g
    hit = half_of == my_half
    chosen, mine = pick(hit, cap)
    _, other = pick(jnp.logical_not(hit), cap)
    valid = jnp.any(chosen, axis=-1)
    mine_rows = jnp.sum(jnp.where(chosen[..., None], row_blocks[:, None], 0), axis=2)
    row_inner = jnp.sum(
        jnp.where(chosen[..., None, None], of_target(inner_of, my_row)[:, None], 0), axis=2
    )
    lanes = jnp.arange(BE)[:, None]
    residues = jnp.arange(g)
    swapped = jnp.logical_not(use_direct(mine[..., None], residues, my_row, my_col))
    tables = {
        "order": order,
        "mine": mine,
        "other": other,
        "valid": valid.astype(jnp.int32),
        "swapped": swapped.astype(jnp.int32).reshape(halves, -1),
        "t_at": (mine_rows // group_count).reshape(halves, -1),
        "u_at": (col_blocks // g).reshape(halves, -1),
        "row_perm": (row_inner[..., None, :] == lanes).astype(BF16),
        "col_perm": (of_target(inner_of, my_col)[..., None, :] == lanes).astype(BF16),
    }

    def of(which):
        return {k: lax.dynamic_index_in_dim(v, which, 0, keepdims=False) for k, v in tables.items()}

    return of(my_half), of(1 - my_half)


def panel_column(received, rows, u_at, my_row, my_col, slots):
    hit = u_at == 0
    found = jnp.any(hit)
    at = jnp.sum(jnp.where(hit, jnp.arange(hit.shape[0]), 0))
    s = at // slots
    k = at % slots
    pieces = []
    for a in range(rows.shape[0]):
        r = rows[a]
        straight = lax.dynamic_slice(received, (r, s, 0, k, 0, 0), (1, 1, slots, 1, BE, BE))[0, 0, :, 0]
        across = lax.dynamic_slice(received, (r, s, k, 0, 0, 0), (1, 1, 1, slots, BE, BE))[0, 0, 0]
        pieces.append(
            jnp.where(use_direct(r, s, my_row, my_col), straight, across.transpose(0, 2, 1))
        )
    return jnp.where(found, jnp.stack(pieces), 0.0)


def panel_add(front_panel, columns, tables, slots):
    row_blocks = front_panel.shape[0]
    hit = (tables["u_at"] == 0).reshape(-1)
    col_perm = jnp.sum(
        jnp.where(hit[:, None, None], tables["col_perm"].reshape(-1, BE, BE).astype(F32), 0.0), axis=0
    )
    moved = jnp.einsum(
        "aixy,aiyz->aixz", tables["row_perm"].astype(F32), columns, precision=HIGHEST
    )
    moved = lax.dot_general(
        moved.reshape(-1, BE), col_perm, NT, precision=HIGHEST
    ).reshape(-1, BE, BE)
    t_of = jnp.where(jnp.repeat(tables["valid"], slots) == 1, tables["t_at"], -1)
    match = t_of[None, :] == jnp.arange(row_blocks)[:, None]
    return front_panel + jnp.sum(
        jnp.where(match[:, :, None, None], moved[None], 0.0), axis=1
    )


def on_device(front_init, child_update, child_map):
    grid_size = lax.axis_size("row")
    halves = lax.axis_size("half")
    group_count = halves * grid_size
    my_half = lax.axis_index("half")
    my_row = lax.axis_index("row")
    my_col = lax.axis_index("col")
    my_group = my_half * grid_size + my_row
    slots = child_update.shape[1] // BE // grid_size
    front_rows, front_cols = front_init.shape
    row_blocks = front_rows // BE
    cap = min(grid_size, row_blocks // slots)
    own, far = all_tables(
        child_map, grid_size, group_count, my_row, my_col, my_half, cap, slots
    )
    orders = own["order"]

    packed = pack(
        child_update[0],
        lax.dynamic_index_in_dim(orders, my_row, 0, keepdims=False),
        lax.dynamic_index_in_dim(orders, my_col, 0, keepdims=False),
        grid_size,
        slots,
    )
    received = exchange(packed, grid_size)

    swap_half = [(0, 1), (1, 0)]
    out_panel = panel_column(received, own["other"], own["u_at"], my_row, my_col, slots)
    far_panel = lax.ppermute(out_panel, "half", swap_half)
    outgoing = jnp.concatenate(
        [lax.dynamic_index_in_dim(received, own["other"][a], 0) for a in range(cap)], axis=0
    )
    outgoing, far_panel = lax.optimization_barrier((outgoing, far_panel))
    incoming = lax.ppermute(outgoing, "half", swap_half)

    own_panel = panel_column(received, own["mine"], own["u_at"], my_row, my_col, slots)
    panel = front_init[:, :BE].reshape(row_blocks, BE, BE)
    panel = panel_add(panel, own_panel, own, slots)
    panel = panel_add(panel, far_panel, far, slots)
    panel = panel.reshape(front_rows, BE)

    slab = lax.all_gather(panel, "col", axis=1, tiled=True)[:, :WIDE]
    diagonal = lax.all_gather(slab[:BE], ("half", "row"), axis=0, tiled=True)[:WIDE]
    pieces = []
    for k in range(grid_size):
        perm = [
            (a * grid_size + q, (q + k) % grid_size * grid_size + a)
            for a in range(grid_size)
            for q in range(grid_size)
        ]
        pieces.append(lax.ppermute(panel, ("row", "col"), perm))
    pieces = jnp.stack(pieces)
    near_rows = jnp.concatenate(
        [
            lax.dynamic_index_in_dim(pieces, (my_row - q) % grid_size, 0, keepdims=False)
            for q in range(WIDE // BE)
        ],
        axis=1,
    ).reshape(row_blocks, BE, WIDE)
    far_rows = lax.ppermute(near_rows, "half", swap_half)
    even = jnp.where(my_half == 0, near_rows, far_rows)
    odd = jnp.where(my_half == 0, far_rows, near_rows)
    column_side = jnp.stack([even, odd], axis=1).reshape(front_cols, WIDE)

    inverse = invert(diagonal)

    def lower(rows, natural):
        full = jnp.dot(rows, inverse.T, precision=HIGHEST)
        second = (jnp.arange(WIDE) >= PANEL)[None, :] & (natural < PANEL)[:, None]
        return jnp.where(second, 0.0, full)

    row_ids = jnp.arange(front_rows)
    natural_rows = (row_ids // BE * group_count + my_group) * BE + row_ids % BE
    col_ids = jnp.arange(front_cols)
    natural_cols = (col_ids // BE * grid_size + my_col) * BE + col_ids % BE
    lrow = lower(slab, natural_rows)
    lcol = lower(column_side, natural_cols)

    chunks = (-1, slots, slots, BE, BE)
    place_of = jnp.stack([my_group, my_col]).astype(jnp.int32)
    at = jnp.minimum(my_col, WIDE // BE - 1) * BE
    lower_col = lax.dynamic_slice_in_dim(lrow, at, BE, axis=1)
    residues = jnp.arange(grid_size)
    front = update(front_init, lrow, lcol)
    front = place(
        front,
        received.reshape(chunks),
        (own["mine"][:, None] * grid_size + residues).reshape(-1),
        own, place_of, lower_col, grid_size, False,
    )
    return place(
        front,
        incoming.reshape(chunks),
        jnp.arange(cap * grid_size),
        far, place_of, lower_col, grid_size, True,
    )


def solution(mesh):
    placed = (P(("half", "row"), "col"), P("half", "row", "col"), P())
    return jax.shard_map(
        on_device, mesh=mesh, in_specs=placed, out_specs=P(("half", "row"), "col"), check_vma=False
    )
```

```python
import functools

import jax
import jax.numpy as jnp
from jax import lax
from jax.experimental import pallas as pl
from jax.experimental.pallas import tpu as pltpu
from jax.sharding import PartitionSpec as P

BE = 128
PANEL = 256
WIDE = 512
HIGHEST = lax.Precision.HIGHEST
F32 = jnp.float32
BF16 = jnp.bfloat16
NT = (((1,), (1,)), ((), ()))


def absdiff(a, b):
    return jnp.maximum(a - b, b - a)


def use_direct(a, b, x, y):
    direct = 2 * absdiff(a, x) + absdiff(b // 2, y // 2)
    swapped = 2 * absdiff(b, x) + absdiff(a // 2, y // 2)
    return direct <= swapped


def pack_kernel(grid_size, slots, row_order, col_order, src, dst):
    for y in range(grid_size):
        for k in range(slots):
            at = pl.multiple_of(col_order[y * slots + k] * BE, BE)
            dst[0, y, 0, k] = src[:, pl.ds(at, BE)]


def pack(child, row_order, col_order, grid_size, slots):
    rows, cols = child.shape
    return pl.pallas_call(
        functools.partial(pack_kernel, grid_size, slots),
        grid_spec=pltpu.PrefetchScalarGridSpec(
            num_scalar_prefetch=2,
            grid=(grid_size * slots,),
            in_specs=[pl.BlockSpec((BE, cols), lambda n, ro, co: (ro[n], 0))],
            out_specs=pl.BlockSpec(
                (1, grid_size, 1, slots, BE, BE),
                lambda n, ro, co: (n // slots, 0, n % slots, 0, 0, 0),
            ),
        ),
        out_shape=jax.ShapeDtypeStruct((grid_size, grid_size, slots, slots, BE, BE), F32),
    )(row_order, col_order, child)


def highest(a, b, dims=(((1,), (0,)), ((), ()))):
    return lax.dot_general(a, b, dims, precision=HIGHEST, preferred_element_type=F32)


def factor_block(work):
    sub = lax.broadcasted_iota(jnp.int32, (BE, 1), 0)
    lane = lax.broadcasted_iota(jnp.int32, (BE, BE), 1)

    def eliminate(j, carry):
        row = work[pl.ds(j, 1), :]
        whole = work[...]
        column = jnp.sum(jnp.where(lane == j, whole[:, :BE], 0.0), axis=1, keepdims=True)
        pivot = jnp.sum(jnp.where(sub == j, column, 0.0), axis=0, keepdims=True)
        root = lax.rsqrt(pivot)
        root = root * (1.5 - 0.5 * pivot * root * root)
        by = jnp.where(sub > j, column * (root * root), jnp.where(sub == j, 1.0 - root, 0.0))
        work[...] = whole - by * row
        return carry

    lax.fori_loop(0, BE, eliminate, 0)


def invert_step(k, schur, inverse, work):
    rows = slice(k * BE, (k + 1) * BE)
    rest = slice((k + 1) * BE, WIDE)
    work[:, :BE] = schur[rows, rows]
    work[:, BE:] = jnp.where(
        lax.broadcasted_iota(jnp.int32, (BE, BE), 0)
        == lax.broadcasted_iota(jnp.int32, (BE, BE), 1),
        1.0,
        0.0,
    ).astype(F32)
    factor_block(work)
    small = work[:, BE:]
    mine = highest(small, inverse[rows, :])
    inverse[rows, :] = mine
    if k + 1 < PANEL_BLOCKS:
        below = highest(schur[rest, rows], small, NT)
        schur[rest, rest] = schur[rest, rest] - highest(below, below, NT)
        inverse[rest, :] = inverse[rest, :] - highest(below, mine)


MESH = pl.DeviceIdType.MESH
PANEL_BLOCKS = WIDE // BE


def remote(source, target, send, recv, device):
    return pltpu.make_async_remote_copy(
        src_ref=source, dst_ref=target, send_sem=send, recv_sem=recv,
        device_id=device, device_id_type=MESH,
    )


class Exchange:
    def __init__(self, g, at, p, src, relay, dst, sems):
        self.g, self.p, self.src, self.relay, self.dst = g, p, src, relay, dst
        self.half, self.r, self.s = at
        (self.send, self.recv, self.relay_send, self.relay_recv, self.local) = sems

    def source(self, kind, x, y):
        return self.src.at[y, x, self.p] if kind else self.src.at[x, y, :, self.p]

    def peer(self, k):
        return (self.r + k // self.g) % self.g, (self.s + k % self.g) % self.g

    def turns(self, x, y):
        return jnp.logical_and(x != self.r, y // 2 != self.s // 2)

    def wanted(self, kind, a, b, x, y):
        if kind:
            return jnp.logical_not(use_direct(b, a, x, y))
        return use_direct(a, b, x, y)

    def first_hop(self, kind, k, x, y):
        g, r, s = self.g, self.r, self.s
        return remote(
            self.source(kind, x, y), self.relay.at[s, x, kind],
            self.send.at[kind * g * g + k], self.relay_recv.at[(s * g + x) * 2 + kind],
            (self.half, r, y),
        )

    def second_hop(self, kind, b, x):
        g, r, s = self.g, self.r, self.s
        target, slot = (
            (self.dst.at[b, r], b * g + r) if kind else (self.dst.at[r, b], r * g + b)
        )
        return remote(
            self.relay.at[b, x, kind], target,
            self.relay_send.at[(b * g + x) * 2 + kind], self.recv.at[slot],
            (self.half, x, s),
        )

    def whole_way(self, kind, k, x, y):
        g, r, s = self.g, self.r, self.s
        target, slot = (
            (self.dst.at[s, r], s * g + r) if kind else (self.dst.at[r, s], r * g + s)
        )
        return remote(
            self.source(kind, x, y), target,
            self.send.at[kind * g * g + k], self.recv.at[slot],
            (self.half, x, y),
        )

    def own(self):
        return pltpu.make_async_copy(
            self.source(0, self.r, self.s), self.dst.at[self.r, self.s], self.local.at[0]
        )

    def own_swap(self):
        return pltpu.make_async_copy(
            self.source(1, self.r, self.s), self.dst.at[self.s, self.r], self.local.at[1]
        )

    def start(self):
        g, r, s = self.g, self.r, self.s
        self.own().start()

        @pl.when(r != s)
        def _():
            self.own_swap().start()

        def turning(k, carry):
            x, y = self.peer(k)
            for kind in range(2):

                @pl.when(jnp.logical_and(self.turns(x, y), self.wanted(kind, r, s, x, y)))
                def _():
                    self.first_hop(kind, k, x, y).start()

            return carry

        lax.fori_loop(1, g * g, turning, 0)

        def straight(k, carry):
            x, y = self.peer(k)
            for kind in range(2):

                @pl.when(
                    jnp.logical_and(
                        jnp.logical_not(self.turns(x, y)), self.wanted(kind, r, s, x, y)
                    )
                )
                def _():
                    self.whole_way(kind, k, x, y).start()

            return carry

        lax.fori_loop(1, g * g, straight, 0)

    def for_relayed(self, act):
        g, r, s = self.g, self.r, self.s

        def one(k, carry):
            x = (r + k // g) % g
            b = (s + g - k % g) % g
            for kind in range(2):

                @pl.when(
                    jnp.logical_and(
                        jnp.logical_and(x != r, b // 2 != s // 2),
                        self.wanted(kind, r, b, x, s),
                    )
                )
                def _():
                    act(kind, b, x)

            return carry

        lax.fori_loop(1, g * g, one, 0)

    def pass_on(self):
        g = self.g

        def act(kind, b, x):
            remote(
                self.source(0, x, b), self.relay.at[b, x, kind],
                self.send.at[0], self.relay_recv.at[(b * g + x) * 2 + kind],
                (self.half, self.r, (self.s + 1) % g),
            ).wait_recv()
            self.second_hop(kind, b, x).start()

        self.for_relayed(act)

    def arrive(self):
        g, r, s = self.g, self.r, self.s

        def arrived(k, carry):
            a, b = k // g, k % g
            mine = jnp.logical_or(
                jnp.logical_and(a == r, b == s), jnp.logical_and(a == s, b == r)
            )

            @pl.when(jnp.logical_not(mine))
            def _():
                remote(
                    self.source(0, a, b), self.dst.at[a, b],
                    self.send.at[0], self.recv.at[k],
                    (self.half, (r + 1) % g, s),
                ).wait_recv()

            return carry

        lax.fori_loop(0, g * g, arrived, 0)
        self.own().wait()

        @pl.when(r != s)
        def _():
            self.own_swap().wait()

    def finish(self):
        g, r, s = self.g, self.r, self.s
        self.for_relayed(lambda kind, b, x: self.second_hop(kind, b, x).wait_send())

        def sent(k, carry):
            x, y = self.peer(k)
            for kind in range(2):

                @pl.when(self.wanted(kind, r, s, x, y))
                def _():
                    self.whole_way(kind, k, x, y).wait_send()

            return carry

        lax.fori_loop(1, g * g, sent, 0)


def exchange_sems(g):
    n = g * g
    return [
        pltpu.SemaphoreType.DMA((2 * n,)),
        pltpu.SemaphoreType.DMA((n,)),
        pltpu.SemaphoreType.DMA((2 * n,)),
        pltpu.SemaphoreType.DMA((2 * n,)),
        pltpu.SemaphoreType.DMA((2,)),
    ]


def position():
    return lax.axis_index("half"), lax.axis_index("row"), lax.axis_index("col")


def greet_half(g, at, barrier):
    half, r, s = at

    def greet(k, carry):
        pl.semaphore_signal(
            barrier, inc=1, device_id=(half, (r + k // g) % g, (s + k % g) % g),
            device_id_type=MESH,
        )
        return carry

    lax.fori_loop(1, g * g, greet, 0)


def first_kernel(g, cap, slots, pick, src, dst, relay, mine, away, whole, give, keep, sems, copy_sem, send, recv):
    at = position()
    half, r, s = at
    barrier = pltpu.get_barrier_semaphore()
    greet_half(g, at, barrier)
    pl.semaphore_signal(barrier, inc=1, device_id=(1 - half, r, s), device_id_type=MESH)
    pl.semaphore_wait(barrier, g * g)
    piece = Exchange(g, at, 0, src, relay, dst, sems)
    piece.start()
    piece.pass_on()
    piece.arrive()
    load = pltpu.make_async_copy(dst, whole, copy_sem)
    load.start()
    load.wait()
    from_col = pick[2 * cap]

    def choose(i, carry):
        for a in range(cap):
            give[a, i] = whole[pick[cap + a], from_col, i]
        return carry

    lax.fori_loop(0, slots, choose, 0)
    over = remote(give, away, send, recv, (1 - half, r, s))
    over.start()

    def hold(i, carry):
        for a in range(cap):
            keep[a, i] = whole[pick[a], from_col, i]
        return carry

    lax.fori_loop(0, slots, hold, 0)
    store = pltpu.make_async_copy(keep, mine, copy_sem)
    store.start()
    store.wait()
    piece.finish()
    over.wait()


def first_exchange(packed, pick, g, cap):
    slots = packed.shape[2]
    blocks = (slots, BE, BE)
    some = (cap,) + blocks
    return pl.pallas_call(
        functools.partial(first_kernel, g, cap, slots),
        out_shape=[
            jax.ShapeDtypeStruct((g, g) + blocks, F32),
            jax.ShapeDtypeStruct((g, g, 2) + blocks, F32),
            jax.ShapeDtypeStruct(some, F32),
            jax.ShapeDtypeStruct(some, F32),
        ],
        in_specs=[
            pl.BlockSpec(memory_space=pltpu.SMEM),
            pl.BlockSpec(memory_space=pl.ANY),
        ],
        out_specs=[pl.BlockSpec(memory_space=pl.ANY)] * 4,
        scratch_shapes=[
            pltpu.VMEM((g, g) + blocks, F32),
            pltpu.VMEM(some, F32),
            pltpu.VMEM(some, F32),
            exchange_sems(g),
            pltpu.SemaphoreType.DMA,
            pltpu.SemaphoreType.DMA,
            pltpu.SemaphoreType.DMA,
        ],
        compiler_params=pltpu.CompilerParams(
            collective_id=0, has_side_effects=True, vmem_limit_bytes=24 * 1024 * 1024
        ),
    )(pick, packed)


def spread_kernel(
    g, cap, slots, pick, src, first, panel,
    recv, relay, incoming, slab, near, far, inverse,
    whole, stage, diagonal, schur, work, sems, copy_sem,
    y_send, y_recv, slab_send, slab_recv, near_send, near_recv,
    far_send, far_recv, diag_send, diag_recv, local,
):
    at = position()
    half, r, s = at
    other = (1 - half, r, s)
    group = half * g + r
    barrier = pltpu.get_barrier_semaphore()
    greet_half(g, at, barrier)

    def greet_other(k, carry):
        pl.semaphore_signal(
            barrier, inc=1, device_id=(1 - half, (r + k) % g, s), device_id_type=MESH
        )
        return carry

    lax.fori_loop(0, g, greet_other, 0)
    pl.semaphore_wait(barrier, g * g - 1 + g)

    holds = s < PANEL_BLOCKS
    at_col = jnp.minimum(s, PANEL_BLOCKS - 1)
    own_slab = pltpu.make_async_copy(panel, slab.at[at_col], local.at[0])
    own_near = pltpu.make_async_copy(panel, near.at[at_col], local.at[1])

    def slab_copy(k):
        return remote(
            panel, slab.at[at_col], slab_send.at[k], slab_recv.at[at_col],
            (half, r, (s + k) % g),
        )

    def near_copy(k):
        return remote(
            panel, near.at[at_col], near_send.at[k], near_recv.at[at_col],
            (half, (r + k) % g, r),
        )

    @pl.when(holds)
    def _():
        own_slab.start()

        def slabs(k, carry):
            slab_copy(k).start()
            return carry

        lax.fori_loop(1, g, slabs, 0)

        @pl.when(s == r)
        def _():
            own_near.start()

        def nears(k, carry):
            @pl.when(jnp.logical_or(k != 0, s != r))
            def _():
                near_copy(k).start()

            return carry

        lax.fori_loop(0, g, nears, 0)

    pieces = [
        Exchange(g, at, q + 1, src, relay.at[q], recv.at[q], sems[q]) for q in range(slots - 1)
    ]

    def over(j):
        return remote(stage.at[j], incoming.at[j], y_send.at[j], y_recv.at[j], other)

    def hand_over(j):
        load = pltpu.make_async_copy(first if j == 0 else recv.at[j - 1], whole, copy_sem)
        load.start()
        load.wait()

        def choose(k, carry):
            for a in range(cap):
                stage[j, a, k // slots, k % slots] = whole[pick[cap + a], k // slots, k % slots]
            return carry

        lax.fori_loop(0, g * slots, choose, 0)
        over(j).start()

    for piece in pieces[:2]:
        piece.start()
    if slots > 1:
        hand_over(0)

    def slab_in(q, carry):
        @pl.when(q != s)
        def _():
            remote(
                panel, slab.at[q], slab_send.at[0], slab_recv.at[q], (half, r, (s + 1) % g)
            ).wait_recv()

        return carry

    lax.fori_loop(0, PANEL_BLOCKS, slab_in, 0)

    @pl.when(holds)
    def _():
        own_slab.wait()

    gives = jnp.logical_and(half == 0, r < PANEL_BLOCKS)
    at_row = jnp.minimum(r, PANEL_BLOCKS - 1)
    top = slab.at[:, pl.ds(0, BE)]
    own_diag = pltpu.make_async_copy(top, diagonal.at[at_row], local.at[2])

    def diag_copy(k):
        to = (group + k) % (2 * g)
        return remote(
            top, diagonal.at[at_row], diag_send.at[k], diag_recv.at[at_row],
            (to // g, to % g, s),
        )

    @pl.when(gives)
    def _():
        own_diag.start()

        def diags(k, carry):
            diag_copy(k).start()
            return carry

        lax.fori_loop(1, 2 * g, diags, 0)

    if pieces:
        pieces[0].pass_on()
    for piece in pieces[2:3]:
        piece.start()

    def near_in(q, carry):
        @pl.when(jnp.logical_not(jnp.logical_and(r == s, q == s)))
        def _():
            remote(
                panel, near.at[q], near_send.at[0], near_recv.at[q], (half, r, (s + 1) % g)
            ).wait_recv()

        return carry

    lax.fori_loop(0, PANEL_BLOCKS, near_in, 0)

    @pl.when(jnp.logical_and(holds, s == r))
    def _():
        own_near.wait()

    far_copy = remote(near, far, far_send, far_recv, other)
    far_copy.start()

    def diag_in(q, carry):
        @pl.when(jnp.logical_not(jnp.logical_and(half == 0, r == q)))
        def _():
            remote(
                top, diagonal.at[q], diag_send.at[0], diag_recv.at[q], other
            ).wait_recv()

        return carry

    lax.fori_loop(0, PANEL_BLOCKS, diag_in, 0)

    @pl.when(gives)
    def _():
        own_diag.wait()

    for a in range(PANEL_BLOCKS):
        for b in range(PANEL_BLOCKS):
            schur[a * BE : (a + 1) * BE, b * BE : (b + 1) * BE] = diagonal[a, b]
    eye = jnp.where(
        lax.broadcasted_iota(jnp.int32, (WIDE, WIDE), 0)
        == lax.broadcasted_iota(jnp.int32, (WIDE, WIDE), 1),
        1.0,
        0.0,
    ).astype(F32)
    inverse[...] = eye
    for k in range(PANEL_BLOCKS):
        invert_step(k, schur, inverse, work)
        if 0 < k < len(pieces):
            pieces[k - 1].arrive()
            if k < slots - 1:
                hand_over(k)
            pieces[k].pass_on()
            for piece in pieces[k + 2 : k + 3]:
                piece.start()
    for k in range(PANEL_BLOCKS, len(pieces)):
        pieces[k - 1].arrive()
        hand_over(k)
        pieces[k].pass_on()
        for piece in pieces[k + 2 : k + 3]:
            piece.start()
    if pieces:
        pieces[-1].arrive()
    for piece in pieces:
        piece.finish()
    for j in range(slots - 1):
        over(j).wait()
    far_copy.wait()

    @pl.when(holds)
    def _():
        def slabs_out(k, carry):
            slab_copy(k).wait_send()
            return carry

        lax.fori_loop(1, g, slabs_out, 0)

        def nears_out(k, carry):
            @pl.when(jnp.logical_or(k != 0, s != r))
            def _():
                near_copy(k).wait_send()

            return carry

        lax.fori_loop(0, g, nears_out, 0)

    @pl.when(gives)
    def _():
        def diags_out(k, carry):
            diag_copy(k).wait_send()
            return carry

        lax.fori_loop(1, 2 * g, diags_out, 0)


def spread(packed, first, panel, pick, g, cap):
    slots = packed.shape[2]
    later = max(slots - 1, 1)
    blocks = (slots, BE, BE)
    slab = (PANEL_BLOCKS,) + panel.shape
    dma = pltpu.SemaphoreType.DMA
    return pl.pallas_call(
        functools.partial(spread_kernel, g, cap, slots),
        out_shape=[
            jax.ShapeDtypeStruct((later, g, g) + blocks, F32),
            jax.ShapeDtypeStruct((later, g, g, 2) + blocks, F32),
            jax.ShapeDtypeStruct((later, cap, g) + blocks, F32),
            jax.ShapeDtypeStruct(slab, F32),
            jax.ShapeDtypeStruct(slab, F32),
            jax.ShapeDtypeStruct(slab, F32),
            jax.ShapeDtypeStruct((WIDE, WIDE), F32),
        ],
        in_specs=[pl.BlockSpec(memory_space=pltpu.SMEM)]
        + [pl.BlockSpec(memory_space=pl.ANY)] * 3,
        out_specs=[pl.BlockSpec(memory_space=pl.ANY)] * 6
        + [pl.BlockSpec(memory_space=pltpu.VMEM)],
        scratch_shapes=[
            pltpu.VMEM((g, g) + blocks, F32),
            pltpu.VMEM((later, cap, g) + blocks, F32),
            pltpu.VMEM((PANEL_BLOCKS, PANEL_BLOCKS, BE, BE), F32),
            pltpu.VMEM((WIDE, WIDE), F32),
            pltpu.VMEM((BE, 2 * BE), F32),
            [exchange_sems(g) for _ in range(later)],
            dma,
            dma((later,)),
            dma((later,)),
            dma((g,)),
            dma((PANEL_BLOCKS,)),
            dma((g,)),
            dma((PANEL_BLOCKS,)),
            dma,
            dma,
            dma((2 * g,)),
            dma((PANEL_BLOCKS,)),
            dma((3,)),
        ],
        compiler_params=pltpu.CompilerParams(
            collective_id=1, has_side_effects=True, vmem_limit_bytes=40 * 1024 * 1024
        ),
    )(pick, packed, first, panel)


def panel_kernel(cap, slots, g, child, t_at, swapped, valid, front, own, far, row_perm, col_perm, out):
    out[...] = front[...]
    for c, blocks in enumerate((own, far)):
        s = child[2 * c]
        perm2 = col_perm[c, s * slots].astype(F32)
        for a in range(cap):
            @pl.when(jnp.logical_and(child[2 * c + 1] == 1, valid[c * cap + a] == 1))
            def _():
                for i in range(slots):
                    t = pl.multiple_of(t_at[(c * cap + a) * slots + i] * BE, BE)
                    perm = row_perm[c, a * slots + i].astype(F32)
                    block = blocks[a, i]
                    turned = swapped[(c * cap + a) * g + s] == 1
                    block = jnp.where(turned, block.T, block)
                    out[pl.ds(t, BE), :] += highest(highest(perm, block), perm2, NT)


def panel_add(front, own, far, t, cap, slots, g):
    rows = front.shape[0]
    perms = lambda x: pl.BlockSpec(x.shape, lambda n, *_: (0, 0, 0, 0))
    return pl.pallas_call(
        functools.partial(panel_kernel, cap, slots, g),
        grid_spec=pltpu.PrefetchScalarGridSpec(
            num_scalar_prefetch=4,
            grid=(1,),
            in_specs=[
                pl.BlockSpec((rows, BE), lambda n, *_: (0, 0)),
                perms(own), perms(far), perms(t["row_perm"]), perms(t["col_perm"]),
            ],
            out_specs=pl.BlockSpec((rows, BE), lambda n, *_: (0, 0)),
        ),
        out_shape=jax.ShapeDtypeStruct((rows, BE), F32),
        compiler_params=pltpu.CompilerParams(vmem_limit_bytes=24 * 1024 * 1024),
    )(t["panel"], t["t_at"], t["swapped"], t["valid"], front, own, far, t["row_perm"], t["col_perm"])


def split(x):
    high = x.astype(BF16)
    return high, (x - high.astype(F32)).astype(BF16)


def place_kernel(
    g, slots, cap, sets, finish, refs_at, child_of, piece_of, a_of, blocks_at,
    t_at, u_at, swapped, valid, place_of, *refs,
):
    front = refs[0]
    chunks = refs[1 : 1 + sets]
    row_perm, col_perm, lower_col, out, acc, mid, sem = refs[1 + sets :]
    n = pl.program_id(0)
    c, p, a = child_of[n], piece_of[n], a_of[n]
    ca = c * cap + a

    @pl.when(n == 0)
    def _():
        load = pltpu.make_async_copy(front, acc, sem)
        load.start()
        load.wait()

    def body(chunk):
        for s in range(g):
            turned = swapped[ca * g + s]

            def moved_rows(i, x, dims):
                high, low = split(x)
                perm = row_perm[c, a * slots + i]
                rows = slice(i * BE, (i + 1) * BE)
                for part, y in enumerate((high, low)):
                    mid[rows, part * BE : (part + 1) * BE] = lax.dot_general(
                        perm, y, dims, preferred_element_type=F32
                    ).astype(BF16)

            @pl.when(turned == 1)
            def _():
                for i in range(slots):
                    moved_rows(i, chunk[0, s, i], NT)

            @pl.when(turned == 0)
            def _():
                for i in range(slots):
                    moved_rows(i, chunk[0, s, i], (((1,), (0,)), ((), ())))

            perm = col_perm[c, s * slots + p]
            moved = lax.dot_general(
                mid[...], jnp.concatenate([perm, perm], axis=1), NT, preferred_element_type=F32
            )
            u = pl.multiple_of(u_at[(c * g + s) * slots + p] * BE, BE)
            for i in range(slots):
                t = pl.multiple_of(t_at[ca * slots + i] * BE, BE)
                acc[pl.ds(t, BE), pl.ds(u, BE)] += moved[i * BE : (i + 1) * BE]

    for m in range(sets):
        @pl.when(jnp.logical_and(refs_at[n] == m, valid[ca] == 1))
        def _():
            body(chunks[m])

    @pl.when(n == pl.num_programs(0) - 1)
    def _():
        if finish:
            @pl.when(place_of[0] < PANEL_BLOCKS)
            def _():
                acc[:BE, :] = jnp.zeros((BE, acc.shape[1]), F32)

            @pl.when(place_of[1] < PANEL_BLOCKS)
            def _():
                acc[:, :BE] = lower_col[...]

        store = pltpu.make_async_copy(acc, out, sem)
        store.start()
        store.wait()


def place(front, sets, steps, t, place_of, lower_col, g, slots, cap, finish):
    which = [step[0] for step in steps]
    held = []
    for m in range(len(sets)):
        now = next(step[1] for step in steps if step[0] == m)
        for step in steps:
            now = step[1] if step[0] == m else now
            held.append(now)
    count = len(steps)
    ints = lambda k: jnp.asarray([step[k] for step in steps], jnp.int32)
    at = jnp.stack([jnp.asarray(x, jnp.int32) for x in held])
    chunk = lambda m: pl.BlockSpec(
        (1, g, slots, BE, BE), lambda n, *refs: (refs[4][m * count + n], 0, 0, 0, 0)
    )
    perms = lambda x: pl.BlockSpec(x.shape, lambda n, *_: (0, 0, 0, 0))
    return pl.pallas_call(
        functools.partial(place_kernel, g, slots, cap, len(sets), finish),
        grid_spec=pltpu.PrefetchScalarGridSpec(
            num_scalar_prefetch=10,
            grid=(count,),
            in_specs=[pl.BlockSpec(memory_space=pl.ANY)]
            + [chunk(m) for m in range(len(sets))]
            + [
                perms(t["row_perm"]),
                perms(t["col_perm"]),
                pl.BlockSpec((front.shape[0], BE), lambda n, *_: (0, 0)),
            ],
            out_specs=pl.BlockSpec(memory_space=pl.ANY),
            scratch_shapes=[
                pltpu.VMEM(front.shape, F32),
                pltpu.VMEM((slots * BE, 2 * BE), BF16),
                pltpu.SemaphoreType.DMA,
            ],
        ),
        out_shape=jax.ShapeDtypeStruct(front.shape, F32),
        compiler_params=pltpu.CompilerParams(vmem_limit_bytes=40 * 1024 * 1024),
        cost_estimate=pl.CostEstimate(
            flops=4_000_000_000, bytes_accessed=36_000_000, transcendentals=0
        ),
    )(
        ints(0), ints(2), ints(3), ints(4), at,
        t["t_at"], t["u_at"], t["swapped"], t["valid"], place_of,
        front, *sets, t["row_perm"], t["col_perm"], lower_col,
    )


def update_kernel(place_of, front, slab, near, far, inverse, out, lower_col, col_high, col_low):
    step = pl.program_id(0)
    half = place_of[2]
    turned = inverse[...]

    def lower(parts, rows):
        return highest(
            jnp.concatenate([parts[q, rows, :] for q in range(PANEL_BLOCKS)], axis=1), turned, NT
        )

    @pl.when(step == 0)
    def _():
        for h, parts in ((half, near), (1 - half, far)):
            for t in range(parts.shape[1] // BE):
                u = pl.multiple_of((2 * t + h) * BE, BE)
                high, low = split(lower(parts, slice(t * BE, (t + 1) * BE)))
                col_high[pl.ds(u, BE), :] = high
                col_low[pl.ds(u, BE), :] = low

    rows = lower(slab, slice(None))
    shown = rows[:, :BE]
    for q in range(1, PANEL_BLOCKS):
        shown = jnp.where(place_of[1] == q, rows[:, q * BE : (q + 1) * BE], shown)
    above = jnp.logical_and(step == 0, place_of[0] < PANEL // BE)
    hidden = jnp.logical_and(above, place_of[1] >= PANEL // BE)
    at = lax.broadcasted_iota(jnp.int32, shown.shape, 0)
    lower_col[...] = jnp.where(jnp.logical_and(hidden, at < BE), 0.0, shown)
    high, low = split(rows)
    width = out.shape[1]
    wide = WIDE if width % WIDE == 0 else 2 * BE
    for at in range(0, width, wide):
        cols = slice(at, at + wide)
        ch = col_high[cols, :]
        total = lax.dot_general(high, ch, NT, preferred_element_type=F32)
        total += lax.dot_general(low, ch, NT, preferred_element_type=F32)
        total += lax.dot_general(high, col_low[cols, :], NT, preferred_element_type=F32)
        out[:, cols] = front[:, cols] - total


def update(front, slab, near, far, inverse, place_of):
    rows, cols = front.shape
    tall = 2 * BE if rows % (2 * BE) == 0 else BE
    whole = pl.BlockSpec(near.shape, lambda t, *_: (0, 0, 0))
    return pl.pallas_call(
        update_kernel,
        grid_spec=pltpu.PrefetchScalarGridSpec(
            num_scalar_prefetch=1,
            grid=(rows // tall,),
            in_specs=[
                pl.BlockSpec((tall, cols), lambda t, *_: (t, 0)),
                pl.BlockSpec((PANEL_BLOCKS, tall, BE), lambda t, *_: (0, t, 0)),
                whole,
                whole,
                pl.BlockSpec((WIDE, WIDE), lambda t, *_: (0, 0)),
            ],
            out_specs=[
                pl.BlockSpec((tall, cols), lambda t, *_: (t, 0)),
                pl.BlockSpec((tall, BE), lambda t, *_: (t, 0)),
            ],
            scratch_shapes=[pltpu.VMEM((cols, WIDE), BF16), pltpu.VMEM((cols, WIDE), BF16)],
        ),
        out_shape=[
            jax.ShapeDtypeStruct(front.shape, F32),
            jax.ShapeDtypeStruct((rows, BE), F32),
        ],
        compiler_params=pltpu.CompilerParams(vmem_limit_bytes=48 * 1024 * 1024),
        cost_estimate=pl.CostEstimate(
            flops=10_000_000_000, bytes_accessed=34_000_000, transcendentals=0
        ),
    )(place_of, front, slab, near, far, inverse)


def pick(hits, count):
    ids = jnp.arange(hits.shape[-1])
    earlier = jnp.logical_and(hits[..., None, :], ids[None, :] < ids[:, None])
    rank = jnp.sum(earlier.astype(jnp.int32), axis=-1)
    chosen = jnp.logical_and(hits[..., None, :], rank[..., None, :] == jnp.arange(count)[:, None])
    return chosen, jnp.sum(jnp.where(chosen, ids, 0), axis=-1)


def all_tables(child_map, grid_size, group_count, my_row, my_col, my_half, cap, slots):
    g, n = grid_size, slots
    halves = child_map.shape[0]
    maps = child_map.reshape(halves, n * g, g, BE).transpose(0, 2, 1, 3)
    block = maps[..., 0] // BE
    inner = maps % BE
    target = block % g
    before = jnp.logical_and(
        target[..., None, :] == target[..., :, None], block[..., None, :] < block[..., :, None]
    )
    at = target * n + jnp.sum(before.astype(jnp.int32), axis=-1)
    hot = at[..., None, :] == jnp.arange(n * g)[:, None]
    order = jnp.sum(jnp.where(hot, jnp.arange(n * g), 0), axis=-1)
    blocks = jnp.sum(jnp.where(hot, block[..., None, :], 0), axis=-1)

    def of_target(x, which):
        return lax.dynamic_slice_in_dim(x, which * n, n, axis=2)

    inner_of = jnp.sum(
        jnp.where(hot[..., None], inner[:, :, None], 0), axis=3
    )
    row_blocks = of_target(blocks, my_row)
    col_blocks = of_target(blocks, my_col)
    half_of = row_blocks[..., 0] % group_count // g
    hit = half_of == my_half
    chosen, mine = pick(hit, cap)
    _, other = pick(jnp.logical_not(hit), cap)
    valid = jnp.any(chosen, axis=-1)
    mine_rows = jnp.sum(jnp.where(chosen[..., None], row_blocks[:, None], 0), axis=2)
    row_inner = jnp.sum(
        jnp.where(chosen[..., None, None], of_target(inner_of, my_row)[:, None], 0), axis=2
    )
    lanes = jnp.arange(BE)[:, None]
    residues = jnp.arange(g)
    swapped = jnp.logical_not(use_direct(mine[..., None], residues, my_row, my_col))
    lead = col_blocks[..., 0] < g
    lead_at = jnp.sum(jnp.where(lead, residues, 0), axis=-1)
    panel = jnp.stack([lead_at, jnp.any(lead, axis=-1).astype(lead_at.dtype)], axis=-1)
    tables = {
        "order": order,
        "pick": jnp.concatenate([mine, other, lead_at[:, None]], axis=1),
        "panel": panel,
        "valid": valid.astype(jnp.int32),
        "swapped": swapped.astype(jnp.int32).reshape(halves, -1),
        "t_at": (mine_rows // group_count).reshape(halves, -1),
        "u_at": (col_blocks // g).reshape(halves, -1),
        "row_perm": (row_inner[..., None, :] == lanes).astype(BF16).reshape(halves, -1, BE, BE),
        "col_perm": (of_target(inner_of, my_col)[..., None, :] == lanes)
        .astype(BF16).reshape(halves, -1, BE, BE),
    }

    flat = ("panel", "valid", "swapped", "t_at", "u_at")

    def own_first(k, v):
        v = jnp.where(my_half == 0, v, v[::-1])
        return v.reshape(-1) if k in flat else v

    return {k: own_first(k, v) for k, v in tables.items()}


def on_device(front_init, child_update, child_map):
    grid_size = lax.axis_size("row")
    halves = lax.axis_size("half")
    group_count = halves * grid_size
    my_half = lax.axis_index("half")
    my_row = lax.axis_index("row")
    my_col = lax.axis_index("col")
    my_group = my_half * grid_size + my_row
    slots = child_update.shape[1] // BE // grid_size
    front_rows, front_cols = front_init.shape
    row_blocks = front_rows // BE
    cap = min(grid_size, row_blocks // slots)
    t = all_tables(
        child_map, grid_size, group_count, my_row, my_col, my_half, cap, slots
    )
    orders = t["order"][0]
    pick = t["pick"][0]
    packed = pack(
        child_update[0],
        lax.dynamic_index_in_dim(orders, my_row, 0, keepdims=False),
        lax.dynamic_index_in_dim(orders, my_col, 0, keepdims=False),
        grid_size,
        slots,
    )
    first, _, own_panel, far_panel = first_exchange(packed, pick, grid_size, cap)
    panel = panel_add(front_init, own_panel, far_panel, t, cap, slots, grid_size)
    recv, _, incoming, slab, near, far, inverse = spread(
        packed, first, panel, pick, grid_size, cap
    )
    last = first if slots == 1 else recv[slots - 2]
    outgoing = jnp.stack(
        [lax.dynamic_index_in_dim(last, pick[cap + a], 0, keepdims=False) for a in range(cap)]
    )
    final = lax.ppermute(outgoing, "half", [(0, 1), (1, 0)])
    place_of = jnp.stack([my_group, my_col, my_half]).astype(jnp.int32)
    front, lower_col = update(front_init, slab, near, far, inverse, place_of)
    chunks = (-1, grid_size, slots, BE, BE)
    mine = [pick[a] for a in range(cap)]
    steps = [(0, mine[a], 0, 0, a) for a in range(cap)]
    sets = [first.reshape(chunks)]
    if slots > 1:
        sets += [recv.reshape(chunks), incoming.reshape(chunks)]
        for p in range(1, slots):
            steps += [(1, (p - 1) * grid_size + mine[a], 0, p, a) for a in range(cap)]
        for p in range(slots - 1):
            steps += [(2, p * cap + a, 1, p, a) for a in range(cap)]
    front = place(
        front, sets, steps, t, place_of, lower_col, grid_size, slots, cap, False
    )
    steps = [(0, a, 1, slots - 1, a) for a in range(cap)]
    return place(
        front, [final.reshape(chunks)], steps, t, place_of, lower_col, grid_size, slots, cap, True
    )


def solution(mesh):
    placed = (P(("half", "row"), "col"), P("half", "row", "col"), P())
    return jax.shard_map(
        on_device, mesh=mesh, in_specs=placed, out_specs=P(("half", "row"), "col"), check_vma=False
    )
```

```python
import functools

import jax
import jax.numpy as jnp
import numpy as np
from jax import lax
from jax.experimental import pallas as pl
from jax.experimental.pallas import tpu as pltpu
from jax.sharding import PartitionSpec as P

BE = 128
PANEL = 256
WIDE = 512
HIGHEST = lax.Precision.HIGHEST
F32 = jnp.float32
BF16 = jnp.bfloat16
NT = (((1,), (1,)), ((), ()))


def absdiff(a, b):
    return jnp.maximum(a - b, b - a)


def use_direct(a, b, x, y):
    direct = 2 * absdiff(a, x) + absdiff(b // 2, y // 2)
    swapped = 2 * absdiff(b, x) + absdiff(a // 2, y // 2)
    return direct <= swapped


def pack_kernel(grid_size, slots, row_order, col_order, src, dst):
    for y in range(grid_size):
        for k in range(slots):
            at = pl.multiple_of(col_order[y * slots + k] * BE, BE)
            dst[0, y, 0, k] = src[:, pl.ds(at, BE)]


def pack(child, row_order, col_order, grid_size, slots):
    rows, cols = child.shape
    return pl.pallas_call(
        functools.partial(pack_kernel, grid_size, slots),
        grid_spec=pltpu.PrefetchScalarGridSpec(
            num_scalar_prefetch=2,
            grid=(grid_size * slots,),
            in_specs=[pl.BlockSpec((BE, cols), lambda n, ro, co: (ro[n], 0))],
            out_specs=pl.BlockSpec(
                (1, grid_size, 1, slots, BE, BE),
                lambda n, ro, co: (n // slots, 0, n % slots, 0, 0, 0),
            ),
        ),
        out_shape=jax.ShapeDtypeStruct((grid_size, grid_size, slots, slots, BE, BE), F32),
    )(row_order, col_order, child)


def highest(a, b, dims=(((1,), (0,)), ((), ()))):
    return lax.dot_general(a, b, dims, precision=HIGHEST, preferred_element_type=F32)


def factor_block(work):
    sub = lax.broadcasted_iota(jnp.int32, (BE, 1), 0)
    lane = lax.broadcasted_iota(jnp.int32, (BE, BE), 1)

    def eliminate(j, carry):
        row = work[pl.ds(j, 1), :]
        whole = work[...]
        column = jnp.sum(jnp.where(lane == j, whole[:, :BE], 0.0), axis=1, keepdims=True)
        pivot = jnp.sum(jnp.where(sub == j, column, 0.0), axis=0, keepdims=True)
        root = lax.rsqrt(pivot)
        root = root * (1.5 - 0.5 * pivot * root * root)
        by = jnp.where(sub > j, column * (root * root), jnp.where(sub == j, 1.0 - root, 0.0))
        work[...] = whole - by * row
        return carry

    lax.fori_loop(0, BE, eliminate, 0)


def invert_step(k, schur, inverse, work):
    rows = slice(k * BE, (k + 1) * BE)
    rest = slice((k + 1) * BE, WIDE)
    work[:, :BE] = schur[rows, rows]
    work[:, BE:] = jnp.where(
        lax.broadcasted_iota(jnp.int32, (BE, BE), 0)
        == lax.broadcasted_iota(jnp.int32, (BE, BE), 1),
        1.0,
        0.0,
    ).astype(F32)
    factor_block(work)
    small = work[:, BE:]
    mine = highest(small, inverse[rows, :])
    inverse[rows, :] = mine
    if k + 1 < PANEL_BLOCKS:
        below = highest(schur[rest, rows], small, NT)
        schur[rest, rest] = schur[rest, rest] - highest(below, below, NT)
        inverse[rest, :] = inverse[rest, :] - highest(below, mine)


MESH = pl.DeviceIdType.MESH
PANEL_BLOCKS = WIDE // BE


def remote(source, target, send, recv, device):
    return pltpu.make_async_remote_copy(
        src_ref=source, dst_ref=target, send_sem=send, recv_sem=recv,
        device_id=device, device_id_type=MESH,
    )


class Exchange:
    def __init__(self, g, at, p, src, relay, dst, sems):
        self.g, self.p, self.src, self.relay, self.dst = g, p, src, relay, dst
        self.half, self.r, self.s = at
        (self.send, self.recv, self.relay_send, self.relay_recv, self.local) = sems

    def source(self, kind, x, y):
        return self.src.at[y, x, self.p] if kind else self.src.at[x, y, :, self.p]

    def peer(self, k):
        return (self.r + k // self.g) % self.g, (self.s + k % self.g) % self.g

    def turns(self, x, y):
        return jnp.logical_and(x != self.r, y // 2 != self.s // 2)

    def wanted(self, kind, a, b, x, y):
        if kind:
            return jnp.logical_not(use_direct(b, a, x, y))
        return use_direct(a, b, x, y)

    def first_hop(self, kind, k, x, y):
        g, r, s = self.g, self.r, self.s
        return remote(
            self.source(kind, x, y), self.relay.at[s, x, kind],
            self.send.at[kind * g * g + k], self.relay_recv.at[(s * g + x) * 2 + kind],
            (self.half, r, y),
        )

    def second_hop(self, kind, b, x):
        g, r, s = self.g, self.r, self.s
        target, slot = (
            (self.dst.at[b, r], b * g + r) if kind else (self.dst.at[r, b], r * g + b)
        )
        return remote(
            self.relay.at[b, x, kind], target,
            self.relay_send.at[(b * g + x) * 2 + kind], self.recv.at[slot],
            (self.half, x, s),
        )

    def whole_way(self, kind, k, x, y):
        g, r, s = self.g, self.r, self.s
        target, slot = (
            (self.dst.at[s, r], s * g + r) if kind else (self.dst.at[r, s], r * g + s)
        )
        return remote(
            self.source(kind, x, y), target,
            self.send.at[kind * g * g + k], self.recv.at[slot],
            (self.half, x, y),
        )

    def own(self):
        return pltpu.make_async_copy(
            self.source(0, self.r, self.s), self.dst.at[self.r, self.s], self.local.at[0]
        )

    def own_swap(self):
        return pltpu.make_async_copy(
            self.source(1, self.r, self.s), self.dst.at[self.s, self.r], self.local.at[1]
        )

    def start(self):
        g, r, s = self.g, self.r, self.s
        self.own().start()

        @pl.when(r != s)
        def _():
            self.own_swap().start()

        def turning(k, carry):
            x, y = self.peer(k)
            for kind in range(2):

                @pl.when(jnp.logical_and(self.turns(x, y), self.wanted(kind, r, s, x, y)))
                def _():
                    self.first_hop(kind, k, x, y).start()

            return carry

        lax.fori_loop(1, g * g, turning, 0)

        def straight(k, carry):
            x, y = self.peer(k)
            for kind in range(2):

                @pl.when(
                    jnp.logical_and(
                        jnp.logical_not(self.turns(x, y)), self.wanted(kind, r, s, x, y)
                    )
                )
                def _():
                    self.whole_way(kind, k, x, y).start()

            return carry

        lax.fori_loop(1, g * g, straight, 0)

    def for_relayed(self, act):
        g, r, s = self.g, self.r, self.s

        def one(k, carry):
            x = (r + k // g) % g
            b = (s + g - k % g) % g
            for kind in range(2):

                @pl.when(
                    jnp.logical_and(
                        jnp.logical_and(x != r, b // 2 != s // 2),
                        self.wanted(kind, r, b, x, s),
                    )
                )
                def _():
                    act(kind, b, x)

            return carry

        lax.fori_loop(1, g * g, one, 0)

    def pass_on(self):
        g = self.g

        def act(kind, b, x):
            remote(
                self.source(0, x, b), self.relay.at[b, x, kind],
                self.send.at[0], self.relay_recv.at[(b * g + x) * 2 + kind],
                (self.half, self.r, (self.s + 1) % g),
            ).wait_recv()
            self.second_hop(kind, b, x).start()

        self.for_relayed(act)

    def arrive(self):
        g, r, s = self.g, self.r, self.s

        def arrived(k, carry):
            a, b = k // g, k % g
            mine = jnp.logical_or(
                jnp.logical_and(a == r, b == s), jnp.logical_and(a == s, b == r)
            )

            @pl.when(jnp.logical_not(mine))
            def _():
                remote(
                    self.source(0, a, b), self.dst.at[a, b],
                    self.send.at[0], self.recv.at[k],
                    (self.half, (r + 1) % g, s),
                ).wait_recv()

            return carry

        lax.fori_loop(0, g * g, arrived, 0)
        self.own().wait()

        @pl.when(r != s)
        def _():
            self.own_swap().wait()

    def finish(self):
        g, r, s = self.g, self.r, self.s
        self.for_relayed(lambda kind, b, x: self.second_hop(kind, b, x).wait_send())

        def sent(k, carry):
            x, y = self.peer(k)
            for kind in range(2):

                @pl.when(self.wanted(kind, r, s, x, y))
                def _():
                    self.whole_way(kind, k, x, y).wait_send()

            return carry

        lax.fori_loop(1, g * g, sent, 0)


def exchange_sems(g):
    n = g * g
    return [
        pltpu.SemaphoreType.DMA((2 * n,)),
        pltpu.SemaphoreType.DMA((n,)),
        pltpu.SemaphoreType.DMA((2 * n,)),
        pltpu.SemaphoreType.DMA((2 * n,)),
        pltpu.SemaphoreType.DMA((2,)),
    ]


def position():
    return lax.axis_index("half"), lax.axis_index("row"), lax.axis_index("col")


def greet_half(g, at, barrier):
    half, r, s = at

    def greet(k, carry):
        pl.semaphore_signal(
            barrier, inc=1, device_id=(half, (r + k // g) % g, (s + k % g) % g),
            device_id_type=MESH,
        )
        return carry

    lax.fori_loop(1, g * g, greet, 0)


def first_kernel(g, cap, slots, pick, src, dst, relay, mine, away, whole, give, keep, sems, copy_sem, send, recv):
    at = position()
    half, r, s = at
    barrier = pltpu.get_barrier_semaphore()
    greet_half(g, at, barrier)
    pl.semaphore_signal(barrier, inc=1, device_id=(1 - half, r, s), device_id_type=MESH)
    pl.semaphore_wait(barrier, g * g)
    piece = Exchange(g, at, 0, src, relay, dst, sems)
    piece.start()
    piece.pass_on()
    piece.arrive()
    load = pltpu.make_async_copy(dst, whole, copy_sem)
    load.start()
    load.wait()
    from_col = pick[2 * cap]

    def choose(i, carry):
        for a in range(cap):
            give[a, i] = whole[pick[cap + a], from_col, i]
        return carry

    lax.fori_loop(0, slots, choose, 0)
    over = remote(give, away, send, recv, (1 - half, r, s))
    over.start()

    def hold(i, carry):
        for a in range(cap):
            keep[a, i] = whole[pick[a], from_col, i]
        return carry

    lax.fori_loop(0, slots, hold, 0)
    store = pltpu.make_async_copy(keep, mine, copy_sem)
    store.start()
    store.wait()
    piece.finish()
    over.wait()


def first_exchange(packed, pick, g, cap):
    slots = packed.shape[2]
    blocks = (slots, BE, BE)
    some = (cap,) + blocks
    return pl.pallas_call(
        functools.partial(first_kernel, g, cap, slots),
        out_shape=[
            jax.ShapeDtypeStruct((g, g) + blocks, F32),
            jax.ShapeDtypeStruct((g, g, 2) + blocks, F32),
            jax.ShapeDtypeStruct(some, F32),
            jax.ShapeDtypeStruct(some, F32),
        ],
        in_specs=[
            pl.BlockSpec(memory_space=pltpu.SMEM),
            pl.BlockSpec(memory_space=pl.ANY),
        ],
        out_specs=[pl.BlockSpec(memory_space=pl.ANY)] * 4,
        scratch_shapes=[
            pltpu.VMEM((g, g) + blocks, F32),
            pltpu.VMEM(some, F32),
            pltpu.VMEM(some, F32),
            exchange_sems(g),
            pltpu.SemaphoreType.DMA,
            pltpu.SemaphoreType.DMA,
            pltpu.SemaphoreType.DMA,
        ],
        compiler_params=pltpu.CompilerParams(
            collective_id=0, has_side_effects=True, vmem_limit_bytes=60 * 1024 * 1024
        ),
    )(pick, packed)


def spread_kernel(
    g, cap, slots, pick, src, first, panel, front,
    recv, relay, incoming, slab, near, far, out, lower_col,
    whole, stage, strip, diagonal, inverse, schur, work, side, col_high, col_low, tiles, done, shown,
    sems, copy_sem,
    y_send, y_recv, slab_send, slab_recv, near_send, near_recv,
    far_send, far_recv, strip_send, strip_recv, diag_send, diag_recv, local, tile_sem, done_sem, shown_sem,
):
    at = position()
    half, r, s = at
    other = (1 - half, r, s)
    group = half * g + r
    barrier = pltpu.get_barrier_semaphore()
    greet_half(g, at, barrier)

    def greet_other(k, carry):
        pl.semaphore_signal(
            barrier, inc=1, device_id=(1 - half, (r + k) % g, s), device_id_type=MESH
        )
        return carry

    lax.fori_loop(0, g, greet_other, 0)
    pl.semaphore_wait(barrier, g * g - 1 + g)

    holds = s < PANEL_BLOCKS
    at_col = jnp.minimum(s, PANEL_BLOCKS - 1)
    own_slab = pltpu.make_async_copy(panel, slab.at[at_col], local.at[0])
    own_near = pltpu.make_async_copy(panel, near.at[at_col], local.at[1])

    def slab_copy(k):
        return remote(
            panel, slab.at[at_col], slab_send.at[k], slab_recv.at[at_col],
            (half, r, (s + k) % g),
        )

    def near_copy(k):
        return remote(
            panel, near.at[at_col], near_send.at[k], near_recv.at[at_col],
            (half, (r + k) % g, r),
        )

    gives = jnp.logical_and(holds, jnp.logical_and(half == 0, r < PANEL_BLOCKS))
    at_row = jnp.minimum(r, PANEL_BLOCKS - 1)
    top = panel.at[pl.ds(0, BE)]
    own_strip = pltpu.make_async_copy(top, strip.at[at_row], local.at[2])
    own_diag = pltpu.make_async_copy(strip, diagonal.at[at_col], local.at[3])

    def strip_copy(k):
        to = (group + k) % (2 * g)
        return remote(
            top, strip.at[at_row], strip_send.at[k], strip_recv.at[at_row],
            (to // g, to % g, s),
        )

    def diag_copy(k):
        return remote(
            strip, diagonal.at[at_col], diag_send.at[k], diag_recv.at[at_col],
            (half, r, (s + k) % g),
        )

    def each(first_k, last_k, act):
        def one(k, carry):
            act(k)
            return carry

        lax.fori_loop(first_k, last_k, one, 0)

    @pl.when(gives)
    def _():
        own_strip.start()
        each(1, 2 * g, lambda k: strip_copy(k).start())

    def strip_in(q):
        @pl.when(jnp.logical_not(jnp.logical_and(half == 0, r == q)))
        def _():
            remote(
                top, strip.at[q], strip_send.at[0], strip_recv.at[q], other
            ).wait_recv()

    @pl.when(holds)
    def _():
        each(0, PANEL_BLOCKS, strip_in)

        @pl.when(gives)
        def _():
            own_strip.wait()

        own_diag.start()
        each(1, g, lambda k: diag_copy(k).start())
        own_slab.start()
        each(1, g, lambda k: slab_copy(k).start())

        @pl.when(s == r)
        def _():
            own_near.start()

        def near_start(k):
            @pl.when(jnp.logical_or(k != 0, s != r))
            def _():
                near_copy(k).start()

        each(0, g, near_start)

    pieces = [
        Exchange(g, at, q + 1, src, relay.at[q], recv.at[q], sems[q]) for q in range(slots - 1)
    ]

    def over(j):
        return remote(stage.at[j], incoming.at[j], y_send.at[j], y_recv.at[j], other)

    def hand_over(j):
        load = pltpu.make_async_copy(first if j == 0 else recv.at[j - 1], whole, copy_sem)
        load.start()
        load.wait()

        def choose(k, carry):
            for a in range(cap):
                stage[j, a, k // slots, k % slots] = whole[pick[cap + a], k // slots, k % slots]
            return carry

        lax.fori_loop(0, g * slots, choose, 0)
        over(j).start()

    for piece in pieces[:2]:
        piece.start()
    if slots > 1:
        hand_over(0)

    def diag_in(q):
        @pl.when(q != s)
        def _():
            remote(
                strip, diagonal.at[q], diag_send.at[0], diag_recv.at[q], (half, r, (s + 1) % g)
            ).wait_recv()

    each(0, PANEL_BLOCKS, diag_in)

    @pl.when(holds)
    def _():
        own_diag.wait()

    for a in range(PANEL_BLOCKS):
        for b in range(PANEL_BLOCKS):
            schur[a * BE : (a + 1) * BE, b * BE : (b + 1) * BE] = diagonal[b, a]
    eye = jnp.where(
        lax.broadcasted_iota(jnp.int32, (WIDE, WIDE), 0)
        == lax.broadcasted_iota(jnp.int32, (WIDE, WIDE), 1),
        1.0,
        0.0,
    ).astype(F32)
    inverse[...] = eye
    far_copy = remote(near, far, far_send, far_recv, other)

    def near_in(q):
        @pl.when(jnp.logical_not(jnp.logical_and(r == s, q == s)))
        def _():
            remote(
                panel, near.at[q], near_send.at[0], near_recv.at[q], (half, r, (s + 1) % g)
            ).wait_recv()

    def nears_in():
        each(0, PANEL_BLOCKS, near_in)

        @pl.when(jnp.logical_and(holds, s == r))
        def _():
            own_near.wait()

        far_copy.start()

    def slab_in(q):
        @pl.when(q != s)
        def _():
            remote(
                panel, slab.at[q], slab_send.at[0], slab_recv.at[q], (half, r, (s + 1) % g)
            ).wait_recv()

    def fetch(array):
        load = pltpu.make_async_copy(array, side, copy_sem)
        load.start()
        load.wait()

    tall = tiles.shape[1]
    count = front.shape[0] // tall

    def lower(t):
        rows = pl.ds(pl.multiple_of(t * tall, tall), tall)
        return highest(
            jnp.concatenate([side[q, rows, :] for q in range(PANEL_BLOCKS)], axis=1),
            inverse[...], NT,
        )

    def column_side(array, h):
        fetch(array)

        def one(t):
            high, low = split(lower(t))
            for k in range(tall // BE):
                at = pl.ds(pl.multiple_of((2 * (t * (tall // BE) + k) + h) * BE, BE), BE)
                col_high[at, :] = high[k * BE : (k + 1) * BE]
                col_low[at, :] = low[k * BE : (k + 1) * BE]

        each(0, count, one)

    def tile_load(t):
        rows = pl.ds(pl.multiple_of(t * tall, tall), tall)
        return pltpu.make_async_copy(front.at[rows], tiles.at[t % 2], tile_sem.at[t % 2])

    def tile_store(t):
        rows = pl.ds(pl.multiple_of(t * tall, tall), tall)
        return pltpu.make_async_copy(done.at[t % 2], out.at[rows], done_sem.at[t % 2])

    def tile(t):
        @pl.when(t + 1 < count)
        def _():
            tile_load(t + 1).start()

        tile_load(t).wait()

        @pl.when(t >= 2)
        def _():
            tile_store(t - 2).wait()

        rows = lower(t)
        mine = rows[:, :BE]
        for q in range(1, PANEL_BLOCKS):
            mine = jnp.where(s == q, rows[:, q * BE : (q + 1) * BE], mine)
        hidden = jnp.logical_and(
            jnp.logical_and(t == 0, group < PANEL // BE), s >= PANEL // BE
        )
        line = lax.broadcasted_iota(jnp.int32, mine.shape, 0)
        shown[pl.ds(pl.multiple_of(t * tall, tall), tall), :] = jnp.where(
            jnp.logical_and(hidden, line < BE), 0.0, mine
        )
        high, low = split(rows)
        width = out.shape[1]
        wide = WIDE if width % WIDE == 0 else 2 * BE
        slot = t % 2
        for at in range(0, width, wide):
            cols = slice(at, at + wide)
            ch = col_high[cols, :]
            total = lax.dot_general(high, ch, NT, preferred_element_type=F32)
            total += lax.dot_general(low, ch, NT, preferred_element_type=F32)
            total += lax.dot_general(high, col_low[cols, :], NT, preferred_element_type=F32)
            done[slot, :, cols] = tiles[slot, :, cols] - total
        tile_store(t).start()

    def advance(k):
        if 0 <= k < len(pieces) - 1:
            pieces[k].arrive()
            hand_over(k + 1)
            pieces[k + 1].pass_on()

    invert_step(0, schur, inverse, work)
    if pieces:
        pieces[0].pass_on()
    invert_step(1, schur, inverse, work)
    nears_in()
    for piece in pieces[2:]:
        piece.start()
    invert_step(2, schur, inverse, work)
    invert_step(3, schur, inverse, work)
    advance(0)
    column_side(near, half)
    far_copy.wait()
    column_side(far, 1 - half)
    each(0, PANEL_BLOCKS, slab_in)

    @pl.when(holds)
    def _():
        own_slab.wait()

    fetch(slab)
    tile_load(0).start()
    each(0, count // 2, tile)
    advance(1)
    each(count // 2, count, tile)
    for k in range(2, slots):
        advance(k)
    tile_store(count - 2).wait()
    tile_store(count - 1).wait()
    shown_store = pltpu.make_async_copy(shown, lower_col, shown_sem)
    shown_store.start()
    if pieces:
        pieces[-1].arrive()
    for piece in pieces:
        piece.finish()
    for j in range(slots - 1):
        over(j).wait()
    shown_store.wait()

    @pl.when(holds)
    def _():
        each(1, g, lambda k: slab_copy(k).wait_send())
        each(1, g, lambda k: diag_copy(k).wait_send())

        def near_out(k):
            @pl.when(jnp.logical_or(k != 0, s != r))
            def _():
                near_copy(k).wait_send()

        each(0, g, near_out)

    @pl.when(gives)
    def _():
        each(1, 2 * g, lambda k: strip_copy(k).wait_send())


def spread(packed, first, panel, front, pick, g, cap):
    slots = packed.shape[2]
    later = max(slots - 1, 1)
    blocks = (slots, BE, BE)
    slab = (PANEL_BLOCKS,) + panel.shape
    rows, cols = front.shape
    tall = 2 * BE if rows % (2 * BE) == 0 else BE
    dma = pltpu.SemaphoreType.DMA
    return pl.pallas_call(
        functools.partial(spread_kernel, g, cap, slots),
        out_shape=[
            jax.ShapeDtypeStruct((later, g, g) + blocks, F32),
            jax.ShapeDtypeStruct((later, g, g, 2) + blocks, F32),
            jax.ShapeDtypeStruct((later, cap, g) + blocks, F32),
            jax.ShapeDtypeStruct(slab, F32),
            jax.ShapeDtypeStruct(slab, F32),
            jax.ShapeDtypeStruct(slab, F32),
            jax.ShapeDtypeStruct(front.shape, F32),
            jax.ShapeDtypeStruct((rows, BE), F32),
        ],
        in_specs=[pl.BlockSpec(memory_space=pltpu.SMEM)]
        + [pl.BlockSpec(memory_space=pl.ANY)] * 4,
        out_specs=[pl.BlockSpec(memory_space=pl.ANY)] * 8,
        scratch_shapes=[
            pltpu.VMEM((g, g) + blocks, F32),
            pltpu.VMEM((later, cap, g) + blocks, F32),
            pltpu.VMEM((PANEL_BLOCKS, BE, BE), F32),
            pltpu.VMEM((PANEL_BLOCKS, PANEL_BLOCKS, BE, BE), F32),
            pltpu.VMEM((WIDE, WIDE), F32),
            pltpu.VMEM((WIDE, WIDE), F32),
            pltpu.VMEM((BE, 2 * BE), F32),
            pltpu.VMEM(slab, F32),
            pltpu.VMEM((cols, WIDE), BF16),
            pltpu.VMEM((cols, WIDE), BF16),
            pltpu.VMEM((2, tall, cols), F32),
            pltpu.VMEM((2, tall, cols), F32),
            pltpu.VMEM((rows, BE), F32),
            [exchange_sems(g) for _ in range(later)],
            dma,
            dma((later,)),
            dma((later,)),
            dma((g,)),
            dma((PANEL_BLOCKS,)),
            dma((g,)),
            dma((PANEL_BLOCKS,)),
            dma,
            dma,
            dma((2 * g,)),
            dma((PANEL_BLOCKS,)),
            dma((g,)),
            dma((PANEL_BLOCKS,)),
            dma((4,)),
            dma((2,)),
            dma((2,)),
            dma,
        ],
        compiler_params=pltpu.CompilerParams(
            collective_id=1, has_side_effects=True, vmem_limit_bytes=60 * 1024 * 1024
        ),
    )(pick, packed, first, panel, front)


def panel_kernel(cap, slots, g, child, t_at, swapped, valid, front, own, far, row_perm, col_perm, out):
    out[...] = front[...]
    for c, blocks in enumerate((own, far)):
        s = child[2 * c]
        perm2 = col_perm[c, s * slots].astype(F32)
        for a in range(cap):
            @pl.when(jnp.logical_and(child[2 * c + 1] == 1, valid[c * cap + a] == 1))
            def _():
                for i in range(slots):
                    t = pl.multiple_of(t_at[(c * cap + a) * slots + i] * BE, BE)
                    perm = row_perm[c, a * slots + i].astype(F32)
                    block = blocks[a, i]
                    turned = swapped[(c * cap + a) * g + s] == 1
                    block = jnp.where(turned, block.T, block)
                    out[pl.ds(t, BE), :] += highest(highest(perm, block), perm2, NT)


def panel_add(front, own, far, t, cap, slots, g):
    rows = front.shape[0]
    perms = lambda x: pl.BlockSpec(x.shape, lambda n, *_: (0, 0, 0, 0))
    return pl.pallas_call(
        functools.partial(panel_kernel, cap, slots, g),
        grid_spec=pltpu.PrefetchScalarGridSpec(
            num_scalar_prefetch=4,
            grid=(1,),
            in_specs=[
                pl.BlockSpec((rows, BE), lambda n, *_: (0, 0)),
                perms(own), perms(far), perms(t["row_perm"]), perms(t["col_perm"]),
            ],
            out_specs=pl.BlockSpec((rows, BE), lambda n, *_: (0, 0)),
        ),
        out_shape=jax.ShapeDtypeStruct((rows, BE), F32),
        compiler_params=pltpu.CompilerParams(vmem_limit_bytes=60 * 1024 * 1024),
    )(t["panel"], t["t_at"], t["swapped"], t["valid"], front, own, far, t["row_perm"], t["col_perm"])


def split(x):
    high = x.astype(BF16)
    return high, (x - high.astype(F32)).astype(BF16)


def place_kernel(
    g, slots, cap, sets, finish, refs_at, child_of, piece_of, a_of, blocks_at,
    t_at, u_at, swapped, valid, place_of, *refs,
):
    front = refs[0]
    chunks = refs[1 : 1 + sets]
    row_perm, col_perm, lower_col, out, acc, mid, sem = refs[1 + sets :]
    n = pl.program_id(0)
    c, p, a = child_of[n], piece_of[n], a_of[n]
    ca = c * cap + a

    @pl.when(n == 0)
    def _():
        load = pltpu.make_async_copy(front, acc, sem)
        load.start()
        load.wait()

    def body(chunk):
        for s in range(g):
            turned = swapped[ca * g + s]

            def moved_rows(i, x, dims):
                high, low = split(x)
                perm = row_perm[c, a * slots + i]
                rows = slice(i * BE, (i + 1) * BE)
                for part, y in enumerate((high, low)):
                    mid[rows, part * BE : (part + 1) * BE] = lax.dot_general(
                        perm, y, dims, preferred_element_type=F32
                    ).astype(BF16)

            @pl.when(turned == 1)
            def _():
                for i in range(slots):
                    moved_rows(i, chunk[0, s, i], NT)

            @pl.when(turned == 0)
            def _():
                for i in range(slots):
                    moved_rows(i, chunk[0, s, i], (((1,), (0,)), ((), ())))

            perm = col_perm[c, s * slots + p]
            moved = lax.dot_general(
                mid[...], jnp.concatenate([perm, perm], axis=1), NT, preferred_element_type=F32
            )
            u = pl.multiple_of(u_at[(c * g + s) * slots + p] * BE, BE)
            for i in range(slots):
                t = pl.multiple_of(t_at[ca * slots + i] * BE, BE)
                acc[pl.ds(t, BE), pl.ds(u, BE)] += moved[i * BE : (i + 1) * BE]

    for m in range(sets):
        @pl.when(jnp.logical_and(refs_at[n] == m, valid[ca] == 1))
        def _():
            body(chunks[m])

    @pl.when(n == pl.num_programs(0) - 1)
    def _():
        if finish:
            @pl.when(place_of[0] < PANEL_BLOCKS)
            def _():
                acc[:BE, :] = jnp.zeros((BE, acc.shape[1]), F32)

            @pl.when(place_of[1] < PANEL_BLOCKS)
            def _():
                acc[:, :BE] = lower_col[...]

        store = pltpu.make_async_copy(acc, out, sem)
        store.start()
        store.wait()


def place(front, sets, steps, mine, t, place_of, lower_col, g, slots, cap, finish):
    held = []
    for m in range(len(sets)):
        now = next(step[1] for step in steps if step[0] == m)
        for step in steps:
            now = step[1] if step[0] == m else now
            held.append(now)
    count = len(steps)
    ints = lambda k: np.asarray([step[k] for step in steps], np.int32)
    base = np.asarray([offset for offset, a in held], np.int32)
    hot = np.asarray([[a == b for b in range(cap)] for offset, a in held], np.int32)
    at = base + jnp.sum(hot * mine, axis=1)
    chunk = lambda m: pl.BlockSpec(
        (1, g, slots, BE, BE), lambda n, *refs: (refs[4][m * count + n], 0, 0, 0, 0)
    )
    perms = lambda x: pl.BlockSpec(x.shape, lambda n, *_: (0, 0, 0, 0))
    return pl.pallas_call(
        functools.partial(place_kernel, g, slots, cap, len(sets), finish),
        grid_spec=pltpu.PrefetchScalarGridSpec(
            num_scalar_prefetch=10,
            grid=(count,),
            in_specs=[pl.BlockSpec(memory_space=pl.ANY)]
            + [chunk(m) for m in range(len(sets))]
            + [
                perms(t["row_perm"]),
                perms(t["col_perm"]),
                pl.BlockSpec((front.shape[0], BE), lambda n, *_: (0, 0)),
            ],
            out_specs=pl.BlockSpec(memory_space=pl.ANY),
            scratch_shapes=[
                pltpu.VMEM(front.shape, F32),
                pltpu.VMEM((slots * BE, 2 * BE), BF16),
                pltpu.SemaphoreType.DMA,
            ],
        ),
        out_shape=jax.ShapeDtypeStruct(front.shape, F32),
        compiler_params=pltpu.CompilerParams(vmem_limit_bytes=60 * 1024 * 1024),
        cost_estimate=pl.CostEstimate(
            flops=4_000_000_000, bytes_accessed=36_000_000, transcendentals=0
        ),
    )(
        ints(0), ints(2), ints(3), ints(4), at,
        t["t_at"], t["u_at"], t["swapped"], t["valid"], place_of,
        front, *sets, t["row_perm"], t["col_perm"], lower_col,
    )


def pick(hits, count):
    ids = jnp.arange(hits.shape[-1])
    earlier = jnp.logical_and(hits[..., None, :], ids[None, :] < ids[:, None])
    rank = jnp.sum(earlier.astype(jnp.int32), axis=-1)
    chosen = jnp.logical_and(hits[..., None, :], rank[..., None, :] == jnp.arange(count)[:, None])
    return chosen, jnp.sum(jnp.where(chosen, ids, 0), axis=-1)


def all_tables(child_map, grid_size, group_count, my_row, my_col, my_half, cap, slots):
    g, n = grid_size, slots
    halves = child_map.shape[0]
    maps = child_map.reshape(halves, n * g, g, BE).transpose(0, 2, 1, 3)
    block = maps[..., 0] // BE
    inner = maps % BE
    target = block % g
    before = jnp.logical_and(
        target[..., None, :] == target[..., :, None], block[..., None, :] < block[..., :, None]
    )
    at = target * n + jnp.sum(before.astype(jnp.int32), axis=-1)
    hot = at[..., None, :] == jnp.arange(n * g)[:, None]
    order = jnp.sum(jnp.where(hot, jnp.arange(n * g), 0), axis=-1)
    blocks = jnp.sum(jnp.where(hot, block[..., None, :], 0), axis=-1)

    def of_target(x, which):
        return lax.dynamic_slice_in_dim(x, which * n, n, axis=2)

    inner_of = jnp.sum(
        jnp.where(hot[..., None], inner[:, :, None], 0), axis=3
    )
    row_blocks = of_target(blocks, my_row)
    col_blocks = of_target(blocks, my_col)
    half_of = row_blocks[..., 0] % group_count // g
    hit = half_of == my_half
    chosen, mine = pick(hit, cap)
    _, other = pick(jnp.logical_not(hit), cap)
    valid = jnp.any(chosen, axis=-1)
    mine_rows = jnp.sum(jnp.where(chosen[..., None], row_blocks[:, None], 0), axis=2)
    row_inner = jnp.sum(
        jnp.where(chosen[..., None, None], of_target(inner_of, my_row)[:, None], 0), axis=2
    )
    lanes = jnp.arange(BE)[:, None]
    residues = jnp.arange(g)
    swapped = jnp.logical_not(use_direct(mine[..., None], residues, my_row, my_col))
    lead = col_blocks[..., 0] < g
    lead_at = jnp.sum(jnp.where(lead, residues, 0), axis=-1)
    panel = jnp.stack([lead_at, jnp.any(lead, axis=-1).astype(lead_at.dtype)], axis=-1)
    tables = {
        "order": order,
        "pick": jnp.concatenate([mine, other, lead_at[:, None]], axis=1),
        "panel": panel,
        "valid": valid.astype(jnp.int32),
        "swapped": swapped.astype(jnp.int32).reshape(halves, -1),
        "t_at": (mine_rows // group_count).reshape(halves, -1),
        "u_at": (col_blocks // g).reshape(halves, -1),
        "row_perm": (row_inner[..., None, :] == lanes).astype(BF16).reshape(halves, -1, BE, BE),
        "col_perm": (of_target(inner_of, my_col)[..., None, :] == lanes)
        .astype(BF16).reshape(halves, -1, BE, BE),
    }

    flat = ("panel", "valid", "swapped", "t_at", "u_at")

    def own_first(k, v):
        v = jnp.where(my_half == 0, v, v[::-1])
        return v.reshape(-1) if k in flat else v

    return {k: own_first(k, v) for k, v in tables.items()}


def on_device(front_init, child_update, child_map):
    grid_size = lax.axis_size("row")
    halves = lax.axis_size("half")
    group_count = halves * grid_size
    my_half = lax.axis_index("half")
    my_row = lax.axis_index("row")
    my_col = lax.axis_index("col")
    my_group = my_half * grid_size + my_row
    slots = child_update.shape[1] // BE // grid_size
    front_rows, front_cols = front_init.shape
    row_blocks = front_rows // BE
    cap = min(grid_size, row_blocks // slots)
    t = all_tables(
        child_map, grid_size, group_count, my_row, my_col, my_half, cap, slots
    )
    orders = t["order"][0]
    pick = t["pick"][0]
    packed = pack(
        child_update[0],
        lax.dynamic_index_in_dim(orders, my_row, 0, keepdims=False),
        lax.dynamic_index_in_dim(orders, my_col, 0, keepdims=False),
        grid_size,
        slots,
    )
    first, _, own_panel, far_panel = first_exchange(packed, pick, grid_size, cap)
    panel = panel_add(front_init, own_panel, far_panel, t, cap, slots, grid_size)
    recv, _, incoming, _, _, _, front, lower_col = spread(
        packed, first, panel, front_init, pick, grid_size, cap
    )
    blocks = (grid_size, slots, BE, BE)

    def chosen(a):
        if slots == 1:
            return lax.dynamic_slice(first, (pick[cap + a], 0, 0, 0, 0), (1,) + blocks)
        return lax.dynamic_slice(
            recv, (slots - 2, pick[cap + a], 0, 0, 0, 0), (1, 1) + blocks
        )[0]

    outgoing = jnp.concatenate([chosen(a) for a in range(cap)], axis=0)
    final = lax.ppermute(outgoing, "half", [(0, 1), (1, 0)])
    place_of = jnp.stack([my_group, my_col]).astype(jnp.int32)
    mine = pick[:cap]
    steps = [(0, (0, a), 0, 0, a) for a in range(cap)]
    sets = [first]
    if slots > 1:
        sets += [recv.reshape((-1,) + blocks), incoming.reshape((-1,) + blocks)]
        for p in range(1, slots):
            steps += [(1, ((p - 1) * grid_size, a), 0, p, a) for a in range(cap)]
        for p in range(slots - 1):
            steps += [(2, (p * cap + a, -1), 1, p, a) for a in range(cap)]
    front = place(
        front, sets, steps, mine, t, place_of, lower_col, grid_size, slots, cap, False
    )
    steps = [(0, (a, -1), 1, slots - 1, a) for a in range(cap)]
    return place(
        front, [final], steps, mine, t, place_of, lower_col, grid_size, slots, cap, True
    )


def solution(mesh):
    placed = (P(("half", "row"), "col"), P("half", "row", "col"), P())
    return jax.shard_map(
        on_device, mesh=mesh, in_specs=placed, out_specs=P(("half", "row"), "col"), check_vma=False
    )
```

```python
import functools

import jax
import jax.numpy as jnp
import numpy as np
from jax import lax
from jax.experimental import pallas as pl
from jax.experimental.pallas import tpu as pltpu
from jax.sharding import PartitionSpec as P

BE = 128
PANEL = 256
WIDE = 512
HIGHEST = lax.Precision.HIGHEST
F32 = jnp.float32
BF16 = jnp.bfloat16
NT = (((1,), (1,)), ((), ()))


def absdiff(a, b):
    return jnp.maximum(a - b, b - a)


def use_direct(a, b, x, y):
    direct = 2 * absdiff(a, x) + absdiff(b // 2, y // 2)
    swapped = 2 * absdiff(b, x) + absdiff(a // 2, y // 2)
    return direct <= swapped


def pack_kernel(grid_size, slots, row_order, col_order, src, dst):
    for y in range(grid_size):
        for k in range(slots):
            at = pl.multiple_of(col_order[y * slots + k] * BE, BE)
            dst[0, y, 0, k] = src[:, pl.ds(at, BE)]


def pack(child, row_order, col_order, grid_size, slots):
    rows, cols = child.shape
    return pl.pallas_call(
        functools.partial(pack_kernel, grid_size, slots),
        grid_spec=pltpu.PrefetchScalarGridSpec(
            num_scalar_prefetch=2,
            grid=(grid_size * slots,),
            in_specs=[pl.BlockSpec((BE, cols), lambda n, ro, co: (ro[n], 0))],
            out_specs=pl.BlockSpec(
                (1, grid_size, 1, slots, BE, BE),
                lambda n, ro, co: (n // slots, 0, n % slots, 0, 0, 0),
            ),
        ),
        out_shape=jax.ShapeDtypeStruct((grid_size, grid_size, slots, slots, BE, BE), F32),
    )(row_order, col_order, child)


def highest(a, b, dims=(((1,), (0,)), ((), ()))):
    return lax.dot_general(a, b, dims, precision=HIGHEST, preferred_element_type=F32)


def factor_block(work):
    sub = lax.broadcasted_iota(jnp.int32, (BE, 1), 0)
    lane = lax.broadcasted_iota(jnp.int32, (BE, BE), 1)

    def eliminate(j, carry):
        row = work[pl.ds(j, 1), :]
        whole = work[...]
        column = jnp.sum(jnp.where(lane == j, whole[:, :BE], 0.0), axis=1, keepdims=True)
        pivot = jnp.sum(jnp.where(sub == j, column, 0.0), axis=0, keepdims=True)
        root = lax.rsqrt(pivot)
        root = root * (1.5 - 0.5 * pivot * root * root)
        by = jnp.where(sub > j, column * (root * root), jnp.where(sub == j, 1.0 - root, 0.0))
        work[...] = whole - by * row
        return carry

    lax.fori_loop(0, BE, eliminate, 0)


def invert_step(k, schur, inverse, work):
    rows = slice(k * BE, (k + 1) * BE)
    rest = slice((k + 1) * BE, WIDE)
    work[:, :BE] = schur[rows, rows]
    work[:, BE:] = jnp.where(
        lax.broadcasted_iota(jnp.int32, (BE, BE), 0)
        == lax.broadcasted_iota(jnp.int32, (BE, BE), 1),
        1.0,
        0.0,
    ).astype(F32)
    factor_block(work)
    small = work[:, BE:]
    mine = highest(small, inverse[rows, :])
    inverse[rows, :] = mine
    if k + 1 < PANEL_BLOCKS:
        below = highest(schur[rest, rows], small, NT)
        schur[rest, rest] = schur[rest, rest] - highest(below, below, NT)
        inverse[rest, :] = inverse[rest, :] - highest(below, mine)


MESH = pl.DeviceIdType.MESH
PANEL_BLOCKS = WIDE // BE


def remote(source, target, send, recv, device):
    return pltpu.make_async_remote_copy(
        src_ref=source, dst_ref=target, send_sem=send, recv_sem=recv,
        device_id=device, device_id_type=MESH,
    )


class Exchange:
    def __init__(self, g, at, p, src, relay, dst, sems):
        self.g, self.p, self.src, self.relay, self.dst = g, p, src, relay, dst
        self.half, self.r, self.s = at
        (self.send, self.recv, self.relay_send, self.relay_recv, self.local) = sems

    def source(self, kind, x, y):
        return self.src.at[y, x, self.p] if kind else self.src.at[x, y, :, self.p]

    def peer(self, k):
        return (self.r + k // self.g) % self.g, (self.s + k % self.g) % self.g

    def turns(self, x, y):
        return jnp.logical_and(x != self.r, y // 2 != self.s // 2)

    def wanted(self, kind, a, b, x, y):
        if kind:
            return jnp.logical_not(use_direct(b, a, x, y))
        return use_direct(a, b, x, y)

    def first_hop(self, kind, k, x, y):
        g, r, s = self.g, self.r, self.s
        return remote(
            self.source(kind, x, y), self.relay.at[s, x, kind],
            self.send.at[kind * g * g + k], self.relay_recv.at[(s * g + x) * 2 + kind],
            (self.half, r, y),
        )

    def second_hop(self, kind, b, x):
        g, r, s = self.g, self.r, self.s
        target, slot = (
            (self.dst.at[b, r], b * g + r) if kind else (self.dst.at[r, b], r * g + b)
        )
        return remote(
            self.relay.at[b, x, kind], target,
            self.relay_send.at[(b * g + x) * 2 + kind], self.recv.at[slot],
            (self.half, x, s),
        )

    def whole_way(self, kind, k, x, y):
        g, r, s = self.g, self.r, self.s
        target, slot = (
            (self.dst.at[s, r], s * g + r) if kind else (self.dst.at[r, s], r * g + s)
        )
        return remote(
            self.source(kind, x, y), target,
            self.send.at[kind * g * g + k], self.recv.at[slot],
            (self.half, x, y),
        )

    def own(self):
        return pltpu.make_async_copy(
            self.source(0, self.r, self.s), self.dst.at[self.r, self.s], self.local.at[0]
        )

    def own_swap(self):
        return pltpu.make_async_copy(
            self.source(1, self.r, self.s), self.dst.at[self.s, self.r], self.local.at[1]
        )

    def start(self):
        g, r, s = self.g, self.r, self.s
        self.own().start()

        @pl.when(r != s)
        def _():
            self.own_swap().start()

        def turning(k, carry):
            x, y = self.peer(k)
            for kind in range(2):

                @pl.when(jnp.logical_and(self.turns(x, y), self.wanted(kind, r, s, x, y)))
                def _():
                    self.first_hop(kind, k, x, y).start()

            return carry

        lax.fori_loop(1, g * g, turning, 0)

        def straight(k, carry):
            x, y = self.peer(k)
            for kind in range(2):

                @pl.when(
                    jnp.logical_and(
                        jnp.logical_not(self.turns(x, y)), self.wanted(kind, r, s, x, y)
                    )
                )
                def _():
                    self.whole_way(kind, k, x, y).start()

            return carry

        lax.fori_loop(1, g * g, straight, 0)

    def for_relayed(self, act):
        g, r, s = self.g, self.r, self.s

        def one(k, carry):
            x = (r + k // g) % g
            b = (s + g - k % g) % g
            for kind in range(2):

                @pl.when(
                    jnp.logical_and(
                        jnp.logical_and(x != r, b // 2 != s // 2),
                        self.wanted(kind, r, b, x, s),
                    )
                )
                def _():
                    act(kind, b, x)

            return carry

        lax.fori_loop(1, g * g, one, 0)

    def pass_on(self):
        g = self.g

        def act(kind, b, x):
            remote(
                self.source(0, x, b), self.relay.at[b, x, kind],
                self.send.at[0], self.relay_recv.at[(b * g + x) * 2 + kind],
                (self.half, self.r, (self.s + 1) % g),
            ).wait_recv()
            self.second_hop(kind, b, x).start()

        self.for_relayed(act)

    def arrive(self):
        g, r, s = self.g, self.r, self.s

        def arrived(k, carry):
            a, b = k // g, k % g
            mine = jnp.logical_or(
                jnp.logical_and(a == r, b == s), jnp.logical_and(a == s, b == r)
            )

            @pl.when(jnp.logical_not(mine))
            def _():
                remote(
                    self.source(0, a, b), self.dst.at[a, b],
                    self.send.at[0], self.recv.at[k],
                    (self.half, (r + 1) % g, s),
                ).wait_recv()

            return carry

        lax.fori_loop(0, g * g, arrived, 0)
        self.own().wait()

        @pl.when(r != s)
        def _():
            self.own_swap().wait()

    def finish(self):
        g, r, s = self.g, self.r, self.s
        self.for_relayed(lambda kind, b, x: self.second_hop(kind, b, x).wait_send())

        def sent(k, carry):
            x, y = self.peer(k)
            for kind in range(2):

                @pl.when(self.wanted(kind, r, s, x, y))
                def _():
                    self.whole_way(kind, k, x, y).wait_send()

            return carry

        lax.fori_loop(1, g * g, sent, 0)


def exchange_sems(g):
    n = g * g
    return [
        pltpu.SemaphoreType.DMA((2 * n,)),
        pltpu.SemaphoreType.DMA((n,)),
        pltpu.SemaphoreType.DMA((2 * n,)),
        pltpu.SemaphoreType.DMA((2 * n,)),
        pltpu.SemaphoreType.DMA((2,)),
    ]


def position():
    return lax.axis_index("half"), lax.axis_index("row"), lax.axis_index("col")


def greet_half(g, at, barrier):
    half, r, s = at

    def greet(k, carry):
        pl.semaphore_signal(
            barrier, inc=1, device_id=(half, (r + k // g) % g, (s + k % g) % g),
            device_id_type=MESH,
        )
        return carry

    lax.fori_loop(1, g * g, greet, 0)


def spread_kernel(
    g, cap, slots, pick, where_at, has, turned, src, front, row_perm, col_perm,
    recv, relay, incoming, slab, near, far, out, lower_col,
    whole, stage, give, held, panel, strip, diagonal, inverse, schur, work, side, col_high, col_low, tiles, done, shown,
    sems, copy_sem,
    y_send, y_recv, slab_send, slab_recv, near_send, near_recv,
    far_send, far_recv, strip_send, strip_recv, diag_send, diag_recv, local, tile_sem, done_sem, shown_sem,
    give_send, give_recv, panel_sem,
):
    at = position()
    half, r, s = at
    other = (1 - half, r, s)
    group = half * g + r
    barrier = pltpu.get_barrier_semaphore()
    greet_half(g, at, barrier)

    def greet_other(k, carry):
        pl.semaphore_signal(
            barrier, inc=1, device_id=(1 - half, (r + k) % g, s), device_id_type=MESH
        )
        return carry

    lax.fori_loop(0, g, greet_other, 0)
    pl.semaphore_wait(barrier, g * g - 1 + g)

    pieces = [
        Exchange(g, at, q, src, relay.at[q], recv.at[q], sems[q]) for q in range(slots)
    ]
    pieces[0].start()
    panel_load = pltpu.make_async_copy(front.at[:, pl.ds(0, BE)], panel, panel_sem)
    panel_load.start()

    def over(j):
        return remote(stage.at[j], incoming.at[j], y_send.at[j], y_recv.at[j], other)

    def each(first_k, last_k, act):
        def one(k, carry):
            act(k)
            return carry

        lax.fori_loop(first_k, last_k, one, 0)

    def take(j):
        load = pltpu.make_async_copy(recv.at[j], whole, copy_sem)
        load.start()
        load.wait()

    def choose(j):
        def one(k):
            for a in range(cap):
                stage[j, a, k // slots, k % slots] = whole[pick[cap + a], k // slots, k % slots]

        each(0, g * slots, one)

    pieces[0].pass_on()
    pieces[0].arrive()
    for piece in pieces[1:2]:
        piece.start()
    take(0)
    lead = pick[2 * cap] // slots

    def choose_panel(i):
        for a in range(cap):
            give[a * slots + i] = whole[pick[cap + a], lead, i]

    each(0, slots, choose_panel)
    give_copy = remote(give, held.at[1], give_send, give_recv, other)
    give_copy.start()

    def hold_panel(i):
        for a in range(cap):
            held[0, a * slots + i] = whole[pick[a], lead, i]

    each(0, slots, hold_panel)
    if slots > 1:
        choose(0)
    panel_load.wait()
    give_copy.wait()
    if slots > 1:
        over(0).start()

    def add_panel(t):
        rows = pl.ds(pl.multiple_of(t * BE, BE), BE)
        total = panel[rows, :]
        for c in range(2):
            at = where_at[c, t]
            block = held[c, at]
            lying = jnp.full((BE, BE), turned[c, t], jnp.int32) == 1
            block = jnp.where(lying, block.T, block)
            moved = highest(
                highest(row_perm[c, at].astype(F32), block),
                col_perm[c, pick[2 * cap + c]].astype(F32), NT,
            )
            total += jnp.where(jnp.full((BE, BE), has[c, t], jnp.int32) == 1, moved, 0.0)
        panel[rows, :] = total

    each(0, panel.shape[0] // BE, add_panel)

    holds = s < PANEL_BLOCKS
    at_col = jnp.minimum(s, PANEL_BLOCKS - 1)
    own_slab = pltpu.make_async_copy(panel, slab.at[at_col], local.at[0])
    own_near = pltpu.make_async_copy(panel, near.at[at_col], local.at[1])

    def slab_copy(k):
        return remote(
            panel, slab.at[at_col], slab_send.at[k], slab_recv.at[at_col],
            (half, r, (s + k) % g),
        )

    def near_copy(k):
        return remote(
            panel, near.at[at_col], near_send.at[k], near_recv.at[at_col],
            (half, (r + k) % g, r),
        )

    gives = jnp.logical_and(holds, jnp.logical_and(half == 0, r < PANEL_BLOCKS))
    at_row = jnp.minimum(r, PANEL_BLOCKS - 1)
    top = panel.at[pl.ds(0, BE)]
    own_strip = pltpu.make_async_copy(top, strip.at[at_row], local.at[2])
    own_diag = pltpu.make_async_copy(strip, diagonal.at[at_col], local.at[3])

    def strip_copy(k):
        to = (group + k) % (2 * g)
        return remote(
            top, strip.at[at_row], strip_send.at[k], strip_recv.at[at_row],
            (to // g, to % g, s),
        )

    def diag_copy(k):
        return remote(
            strip, diagonal.at[at_col], diag_send.at[k], diag_recv.at[at_col],
            (half, r, (s + k) % g),
        )

    @pl.when(gives)
    def _():
        own_strip.start()
        each(1, 2 * g, lambda k: strip_copy(k).start())

    def strip_in(q):
        @pl.when(jnp.logical_not(jnp.logical_and(half == 0, r == q)))
        def _():
            remote(
                top, strip.at[q], strip_send.at[0], strip_recv.at[q], other
            ).wait_recv()

    @pl.when(holds)
    def _():
        each(0, PANEL_BLOCKS, strip_in)

        @pl.when(gives)
        def _():
            own_strip.wait()

        own_diag.start()
        each(1, g, lambda k: diag_copy(k).start())
        own_slab.start()
        each(1, g, lambda k: slab_copy(k).start())

        @pl.when(s == r)
        def _():
            own_near.start()

        def near_start(k):
            @pl.when(jnp.logical_or(k != 0, s != r))
            def _():
                near_copy(k).start()

        each(0, g, near_start)

    def hand_over(j):
        take(j)
        choose(j)
        over(j).start()

    if slots > 1:
        pieces[1].pass_on()

    def diag_in(q):
        @pl.when(q != s)
        def _():
            remote(
                strip, diagonal.at[q], diag_send.at[0], diag_recv.at[q], (half, r, (s + 1) % g)
            ).wait_recv()

    each(0, PANEL_BLOCKS, diag_in)

    @pl.when(holds)
    def _():
        own_diag.wait()

    for a in range(PANEL_BLOCKS):
        for b in range(PANEL_BLOCKS):
            schur[a * BE : (a + 1) * BE, b * BE : (b + 1) * BE] = diagonal[b, a]
    eye = jnp.where(
        lax.broadcasted_iota(jnp.int32, (WIDE, WIDE), 0)
        == lax.broadcasted_iota(jnp.int32, (WIDE, WIDE), 1),
        1.0,
        0.0,
    ).astype(F32)
    inverse[...] = eye
    far_copy = remote(near, far, far_send, far_recv, other)

    def near_in(q):
        @pl.when(jnp.logical_not(jnp.logical_and(r == s, q == s)))
        def _():
            remote(
                panel, near.at[q], near_send.at[0], near_recv.at[q], (half, r, (s + 1) % g)
            ).wait_recv()

    def nears_in():
        each(0, PANEL_BLOCKS, near_in)

        @pl.when(jnp.logical_and(holds, s == r))
        def _():
            own_near.wait()

        far_copy.start()

    def slab_in(q):
        @pl.when(q != s)
        def _():
            remote(
                panel, slab.at[q], slab_send.at[0], slab_recv.at[q], (half, r, (s + 1) % g)
            ).wait_recv()

    def fetch(array):
        load = pltpu.make_async_copy(array, side, copy_sem)
        load.start()
        load.wait()

    tall = tiles.shape[1]
    count = front.shape[0] // tall

    def lower(t):
        rows = pl.ds(pl.multiple_of(t * tall, tall), tall)
        return highest(
            jnp.concatenate([side[q, rows, :] for q in range(PANEL_BLOCKS)], axis=1),
            inverse[...], NT,
        )

    def column_side(array, h):
        fetch(array)

        def one(t):
            high, low = split(lower(t))
            for k in range(tall // BE):
                at = pl.ds(pl.multiple_of((2 * (t * (tall // BE) + k) + h) * BE, BE), BE)
                col_high[at, :] = high[k * BE : (k + 1) * BE]
                col_low[at, :] = low[k * BE : (k + 1) * BE]

        each(0, count, one)

    def tile_load(t):
        rows = pl.ds(pl.multiple_of(t * tall, tall), tall)
        return pltpu.make_async_copy(front.at[rows], tiles.at[t % 2], tile_sem.at[t % 2])

    def tile_store(t):
        rows = pl.ds(pl.multiple_of(t * tall, tall), tall)
        return pltpu.make_async_copy(done.at[t % 2], out.at[rows], done_sem.at[t % 2])

    def tile(t):
        @pl.when(t + 1 < count)
        def _():
            tile_load(t + 1).start()

        tile_load(t).wait()

        @pl.when(t >= 2)
        def _():
            tile_store(t - 2).wait()

        rows = lower(t)
        mine = rows[:, :BE]
        for q in range(1, PANEL_BLOCKS):
            mine = jnp.where(s == q, rows[:, q * BE : (q + 1) * BE], mine)
        hidden = jnp.logical_and(
            jnp.logical_and(t == 0, group < PANEL // BE), s >= PANEL // BE
        )
        line = lax.broadcasted_iota(jnp.int32, mine.shape, 0)
        shown[pl.ds(pl.multiple_of(t * tall, tall), tall), :] = jnp.where(
            jnp.logical_and(hidden, line < BE), 0.0, mine
        )
        high, low = split(rows)
        width = out.shape[1]
        wide = WIDE if width % WIDE == 0 else 2 * BE
        slot = t % 2
        for at in range(0, width, wide):
            cols = slice(at, at + wide)
            ch = col_high[cols, :]
            total = lax.dot_general(high, ch, NT, preferred_element_type=F32)
            total += lax.dot_general(low, ch, NT, preferred_element_type=F32)
            total += lax.dot_general(high, col_low[cols, :], NT, preferred_element_type=F32)
            done[slot, :, cols] = tiles[slot, :, cols] - total
        tile_store(t).start()

    def advance(k):
        if 0 < k < slots - 1:
            pieces[k].arrive()
            hand_over(k)
            pieces[k + 1].pass_on()

    invert_step(0, schur, inverse, work)
    nears_in()
    for piece in pieces[2:3]:
        piece.start()
    invert_step(1, schur, inverse, work)
    for piece in pieces[3:]:
        piece.start()
    advance(1)
    invert_step(2, schur, inverse, work)
    invert_step(3, schur, inverse, work)
    column_side(near, half)
    far_copy.wait()
    column_side(far, 1 - half)
    advance(2)
    each(0, PANEL_BLOCKS, slab_in)

    @pl.when(holds)
    def _():
        own_slab.wait()

    fetch(slab)
    tile_load(0).start()
    each(0, count, tile)
    for k in range(3, slots):
        advance(k)
    tile_store(count - 2).wait()
    tile_store(count - 1).wait()
    shown_store = pltpu.make_async_copy(shown, lower_col, shown_sem)
    shown_store.start()
    if slots > 1:
        pieces[-1].arrive()
    for piece in pieces:
        piece.finish()
    for j in range(slots - 1):
        over(j).wait()
    shown_store.wait()

    @pl.when(holds)
    def _():
        each(1, g, lambda k: slab_copy(k).wait_send())
        each(1, g, lambda k: diag_copy(k).wait_send())

        def near_out(k):
            @pl.when(jnp.logical_or(k != 0, s != r))
            def _():
                near_copy(k).wait_send()

        each(0, g, near_out)

    @pl.when(gives)
    def _():
        each(1, 2 * g, lambda k: strip_copy(k).wait_send())


def spread(packed, front, t, g, cap):
    slots = packed.shape[2]
    later = max(slots - 1, 1)
    blocks = (slots, BE, BE)
    rows, cols = front.shape
    slab = (PANEL_BLOCKS, rows, BE)
    tall = 2 * BE if rows % (2 * BE) == 0 else BE
    dma = pltpu.SemaphoreType.DMA
    return pl.pallas_call(
        functools.partial(spread_kernel, g, cap, slots),
        out_shape=[
            jax.ShapeDtypeStruct((slots, g, g) + blocks, F32),
            jax.ShapeDtypeStruct((slots, g, g, 2) + blocks, F32),
            jax.ShapeDtypeStruct((later, cap, g) + blocks, F32),
            jax.ShapeDtypeStruct(slab, F32),
            jax.ShapeDtypeStruct(slab, F32),
            jax.ShapeDtypeStruct(slab, F32),
            jax.ShapeDtypeStruct(front.shape, F32),
            jax.ShapeDtypeStruct((rows, BE), F32),
        ],
        in_specs=[pl.BlockSpec(memory_space=pltpu.SMEM)] * 4
        + [pl.BlockSpec(memory_space=pl.ANY)] * 2
        + [pl.BlockSpec(memory_space=pltpu.VMEM)] * 2,
        out_specs=[pl.BlockSpec(memory_space=pl.ANY)] * 8,
        scratch_shapes=[
            pltpu.VMEM((g, g) + blocks, F32),
            pltpu.VMEM((later, cap, g) + blocks, F32),
            pltpu.VMEM((cap * slots, BE, BE), F32),
            pltpu.VMEM((2, cap * slots, BE, BE), F32),
            pltpu.VMEM((rows, BE), F32),
            pltpu.VMEM((PANEL_BLOCKS, BE, BE), F32),
            pltpu.VMEM((PANEL_BLOCKS, PANEL_BLOCKS, BE, BE), F32),
            pltpu.VMEM((WIDE, WIDE), F32),
            pltpu.VMEM((WIDE, WIDE), F32),
            pltpu.VMEM((BE, 2 * BE), F32),
            pltpu.VMEM(slab, F32),
            pltpu.VMEM((cols, WIDE), BF16),
            pltpu.VMEM((cols, WIDE), BF16),
            pltpu.VMEM((2, tall, cols), F32),
            pltpu.VMEM((2, tall, cols), F32),
            pltpu.VMEM((rows, BE), F32),
            [exchange_sems(g) for _ in range(slots)],
            dma,
            dma((later,)),
            dma((later,)),
            dma((g,)),
            dma((PANEL_BLOCKS,)),
            dma((g,)),
            dma((PANEL_BLOCKS,)),
            dma,
            dma,
            dma((2 * g,)),
            dma((PANEL_BLOCKS,)),
            dma((g,)),
            dma((PANEL_BLOCKS,)),
            dma((4,)),
            dma((2,)),
            dma((2,)),
            dma,
            dma,
            dma,
            dma,
        ],
        compiler_params=pltpu.CompilerParams(
            collective_id=0, has_side_effects=True, vmem_limit_bytes=60 * 1024 * 1024
        ),
    )(
        t["pick"], t["where_at"], t["has"], t["turned"], packed, front, t["row_perm"], t["col_perm"]
    )


def split(x):
    high = x.astype(BF16)
    return high, (x - high.astype(F32)).astype(BF16)


def place_kernel(
    g, slots, cap, sets, finish, refs_at, child_of, piece_of, a_of, blocks_at,
    t_at, u_at, swapped, valid, place_of, *refs,
):
    front = refs[0]
    chunks = refs[1 : 1 + sets]
    row_perm, col_perm, lower_col, out, acc, mid, sem = refs[1 + sets :]
    n = pl.program_id(0)
    c, p, a = child_of[n], piece_of[n], a_of[n]
    ca = c * cap + a

    @pl.when(n == 0)
    def _():
        load = pltpu.make_async_copy(front, acc, sem)
        load.start()
        load.wait()

    def body(chunk):
        for s in range(g):
            turned = swapped[ca * g + s]

            def moved_rows(i, x, dims):
                high, low = split(x)
                perm = row_perm[c, a * slots + i]
                rows = slice(i * BE, (i + 1) * BE)
                for part, y in enumerate((high, low)):
                    mid[rows, part * BE : (part + 1) * BE] = lax.dot_general(
                        perm, y, dims, preferred_element_type=F32
                    ).astype(BF16)

            @pl.when(turned == 1)
            def _():
                for i in range(slots):
                    moved_rows(i, chunk[0, s, i], NT)

            @pl.when(turned == 0)
            def _():
                for i in range(slots):
                    moved_rows(i, chunk[0, s, i], (((1,), (0,)), ((), ())))

            perm = col_perm[c, s * slots + p]
            moved = lax.dot_general(
                mid[...], jnp.concatenate([perm, perm], axis=1), NT, preferred_element_type=F32
            )
            u = pl.multiple_of(u_at[(c * g + s) * slots + p] * BE, BE)
            for i in range(slots):
                t = pl.multiple_of(t_at[ca * slots + i] * BE, BE)
                acc[pl.ds(t, BE), pl.ds(u, BE)] += moved[i * BE : (i + 1) * BE]

    for m in range(sets):
        @pl.when(jnp.logical_and(refs_at[n] == m, valid[ca] == 1))
        def _():
            body(chunks[m])

    @pl.when(n == pl.num_programs(0) - 1)
    def _():
        if finish:
            @pl.when(place_of[0] < PANEL_BLOCKS)
            def _():
                acc[:BE, :] = jnp.zeros((BE, acc.shape[1]), F32)

            @pl.when(place_of[1] < PANEL_BLOCKS)
            def _():
                acc[:, :BE] = lower_col[...]

        store = pltpu.make_async_copy(acc, out, sem)
        store.start()
        store.wait()


def place(front, sets, steps, mine, t, place_of, lower_col, g, slots, cap, finish):
    held = []
    for m in range(len(sets)):
        now = next(step[1] for step in steps if step[0] == m)
        for step in steps:
            now = step[1] if step[0] == m else now
            held.append(now)
    count = len(steps)
    ints = lambda k: np.asarray([step[k] for step in steps], np.int32)
    base = np.asarray([offset for offset, a in held], np.int32)
    hot = np.asarray([[a == b for b in range(cap)] for offset, a in held], np.int32)
    at = base + jnp.sum(hot * mine, axis=1)
    chunk = lambda m: pl.BlockSpec(
        (1, g, slots, BE, BE), lambda n, *refs: (refs[4][m * count + n], 0, 0, 0, 0)
    )
    perms = lambda x: pl.BlockSpec(x.shape, lambda n, *_: (0, 0, 0, 0))
    return pl.pallas_call(
        functools.partial(place_kernel, g, slots, cap, len(sets), finish),
        grid_spec=pltpu.PrefetchScalarGridSpec(
            num_scalar_prefetch=10,
            grid=(count,),
            in_specs=[pl.BlockSpec(memory_space=pl.ANY)]
            + [chunk(m) for m in range(len(sets))]
            + [
                perms(t["row_perm"]),
                perms(t["col_perm"]),
                pl.BlockSpec((front.shape[0], BE), lambda n, *_: (0, 0)),
            ],
            out_specs=pl.BlockSpec(memory_space=pl.ANY),
            scratch_shapes=[
                pltpu.VMEM(front.shape, F32),
                pltpu.VMEM((slots * BE, 2 * BE), BF16),
                pltpu.SemaphoreType.DMA,
            ],
        ),
        out_shape=jax.ShapeDtypeStruct(front.shape, F32),
        compiler_params=pltpu.CompilerParams(vmem_limit_bytes=60 * 1024 * 1024),
        cost_estimate=pl.CostEstimate(
            flops=4_000_000_000, bytes_accessed=36_000_000, transcendentals=0
        ),
    )(
        ints(0), ints(2), ints(3), ints(4), at,
        t["t_at"], t["u_at"], t["swapped"], t["valid"], place_of,
        front, *sets, t["row_perm"], t["col_perm"], lower_col,
    )


def pick(hits, count):
    ids = jnp.arange(hits.shape[-1])
    earlier = jnp.logical_and(hits[..., None, :], ids[None, :] < ids[:, None])
    rank = jnp.sum(earlier.astype(jnp.int32), axis=-1)
    chosen = jnp.logical_and(hits[..., None, :], rank[..., None, :] == jnp.arange(count)[:, None])
    return chosen, jnp.sum(jnp.where(chosen, ids, 0), axis=-1)


def all_tables(
    child_map, grid_size, group_count, my_row, my_col, my_half, cap, slots, row_blocks_count
):
    g, n = grid_size, slots
    halves = child_map.shape[0]
    maps = child_map.reshape(halves, n * g, g, BE).transpose(0, 2, 1, 3)
    block = maps[..., 0] // BE
    inner = maps % BE
    target = block % g
    before = jnp.logical_and(
        target[..., None, :] == target[..., :, None], block[..., None, :] < block[..., :, None]
    )
    at = target * n + jnp.sum(before.astype(jnp.int32), axis=-1)
    hot = at[..., None, :] == jnp.arange(n * g)[:, None]
    order = jnp.sum(jnp.where(hot, jnp.arange(n * g), 0), axis=-1)
    blocks = jnp.sum(jnp.where(hot, block[..., None, :], 0), axis=-1)

    def of_target(x, which):
        return lax.dynamic_slice_in_dim(x, which * n, n, axis=2)

    inner_of = jnp.sum(
        jnp.where(hot[..., None], inner[:, :, None], 0), axis=3
    )
    row_blocks = of_target(blocks, my_row)
    col_blocks = of_target(blocks, my_col)
    half_of = row_blocks[..., 0] % group_count // g
    hit = half_of == my_half
    chosen, mine = pick(hit, cap)
    _, other = pick(jnp.logical_not(hit), cap)
    valid = jnp.any(chosen, axis=-1)
    mine_rows = jnp.sum(jnp.where(chosen[..., None], row_blocks[:, None], 0), axis=2)
    row_inner = jnp.sum(
        jnp.where(chosen[..., None, None], of_target(inner_of, my_row)[:, None], 0), axis=2
    )
    lanes = jnp.arange(BE)[:, None]
    residues = jnp.arange(g)
    swapped = jnp.logical_not(use_direct(mine[..., None], residues, my_row, my_col))
    lead = col_blocks[..., 0] < g
    lead_at = jnp.sum(jnp.where(lead, residues, 0), axis=-1)
    fits = jnp.logical_and(
        (mine_rows // group_count)[..., None] == jnp.arange(row_blocks_count),
        jnp.logical_and(valid, jnp.any(lead, axis=-1)[:, None])[..., None, None],
    )
    block_id = (jnp.arange(cap)[:, None] * n + jnp.arange(n))[..., None]
    across = jnp.logical_not(use_direct(mine, lead_at[:, None], my_row, my_col))
    tables = {
        "order": order,
        "picks": jnp.concatenate([mine, other], axis=1),
        "leads": lead_at * n,
        "where_at": jnp.sum(jnp.where(fits, block_id, 0), axis=(1, 2)),
        "has": jnp.sum(fits.astype(jnp.int32), axis=(1, 2)),
        "turned": jnp.sum(
            jnp.logical_and(fits, across[..., None, None]).astype(jnp.int32), axis=(1, 2)
        ),
        "valid": valid.astype(jnp.int32),
        "swapped": swapped.astype(jnp.int32).reshape(halves, -1),
        "t_at": (mine_rows // group_count).reshape(halves, -1),
        "u_at": (col_blocks // g).reshape(halves, -1),
        "row_perm": (row_inner[..., None, :] == lanes).astype(BF16).reshape(halves, -1, BE, BE),
        "col_perm": (of_target(inner_of, my_col)[..., None, :] == lanes)
        .astype(BF16).reshape(halves, -1, BE, BE),
    }

    flat = ("valid", "swapped", "t_at", "u_at")

    def own_first(k, v):
        v = jnp.where(my_half == 0, v, v[::-1])
        return v.reshape(-1) if k in flat else v

    t = {k: own_first(k, v) for k, v in tables.items()}
    t["pick"] = jnp.concatenate([t["picks"][0], t["leads"]])
    return t


def on_device(front_init, child_update, child_map):
    grid_size = lax.axis_size("row")
    halves = lax.axis_size("half")
    group_count = halves * grid_size
    my_half = lax.axis_index("half")
    my_row = lax.axis_index("row")
    my_col = lax.axis_index("col")
    my_group = my_half * grid_size + my_row
    slots = child_update.shape[1] // BE // grid_size
    front_rows, front_cols = front_init.shape
    row_blocks = front_rows // BE
    cap = min(grid_size, row_blocks // slots)
    t = all_tables(
        child_map, grid_size, group_count, my_row, my_col, my_half, cap, slots, row_blocks
    )
    orders = t["order"][0]
    pick = t["pick"]
    packed = pack(
        child_update[0],
        lax.dynamic_index_in_dim(orders, my_row, 0, keepdims=False),
        lax.dynamic_index_in_dim(orders, my_col, 0, keepdims=False),
        grid_size,
        slots,
    )
    recv, _, incoming, _, _, _, front, lower_col = spread(packed, front_init, t, grid_size, cap)
    blocks = (grid_size, slots, BE, BE)

    def chosen(a):
        return lax.dynamic_slice(
            recv, (slots - 1, pick[cap + a], 0, 0, 0, 0), (1, 1) + blocks
        )[0]

    outgoing = jnp.concatenate([chosen(a) for a in range(cap)], axis=0)
    final = lax.ppermute(outgoing, "half", [(0, 1), (1, 0)])
    place_of = jnp.stack([my_group, my_col]).astype(jnp.int32)
    mine = pick[:cap]
    sets = [recv.reshape((-1,) + blocks), incoming.reshape((-1,) + blocks)]
    steps = []
    for p in range(slots):
        steps += [(0, (p * grid_size, a), 0, p, a) for a in range(cap)]
    for p in range(slots - 1):
        steps += [(1, (p * cap + a, -1), 1, p, a) for a in range(cap)]
    if slots == 1:
        sets = sets[:1]
    front = place(
        front, sets, steps, mine, t, place_of, lower_col, grid_size, slots, cap, False
    )
    steps = [(0, (a, -1), 1, slots - 1, a) for a in range(cap)]
    return place(
        front, [final], steps, mine, t, place_of, lower_col, grid_size, slots, cap, True
    )


def solution(mesh):
    placed = (P(("half", "row"), "col"), P("half", "row", "col"), P())
    return jax.shard_map(
        on_device, mesh=mesh, in_specs=placed, out_specs=P(("half", "row"), "col"), check_vma=False
    )
```

```python
import functools

import jax
import jax.numpy as jnp
import numpy as np
from jax import lax
from jax.experimental import pallas as pl
from jax.experimental.pallas import tpu as pltpu
from jax.sharding import PartitionSpec as P

BE = 128
PANEL = 256
WIDE = 512
HIGHEST = lax.Precision.HIGHEST
F32 = jnp.float32
BF16 = jnp.bfloat16
NT = (((1,), (1,)), ((), ()))


def absdiff(a, b):
    return jnp.maximum(a - b, b - a)


def use_direct(a, b, x, y):
    direct = 2 * absdiff(a, x) + absdiff(b // 2, y // 2)
    swapped = 2 * absdiff(b, x) + absdiff(a // 2, y // 2)
    return direct <= swapped


def pack_kernel(grid_size, slots, row_order, col_order, src, dst):
    for y in range(grid_size):
        for k in range(slots):
            at = pl.multiple_of(col_order[y * slots + k] * BE, BE)
            dst[0, y, 0, k] = src[:, pl.ds(at, BE)]


def pack(child, row_order, col_order, grid_size, slots):
    rows, cols = child.shape
    return pl.pallas_call(
        functools.partial(pack_kernel, grid_size, slots),
        grid_spec=pltpu.PrefetchScalarGridSpec(
            num_scalar_prefetch=2,
            grid=(grid_size * slots,),
            in_specs=[pl.BlockSpec((BE, cols), lambda n, ro, co: (ro[n], 0))],
            out_specs=pl.BlockSpec(
                (1, grid_size, 1, slots, BE, BE),
                lambda n, ro, co: (n // slots, 0, n % slots, 0, 0, 0),
            ),
        ),
        out_shape=jax.ShapeDtypeStruct((grid_size, grid_size, slots, slots, BE, BE), F32),
    )(row_order, col_order, child)


def highest(a, b, dims=(((1,), (0,)), ((), ()))):
    return lax.dot_general(a, b, dims, precision=HIGHEST, preferred_element_type=F32)


def factor_block(work):
    sub = lax.broadcasted_iota(jnp.int32, (BE, 1), 0)
    lane = lax.broadcasted_iota(jnp.int32, (BE, BE), 1)

    def eliminate(j, carry):
        row = work[pl.ds(j, 1), :]
        whole = work[...]
        column = jnp.sum(jnp.where(lane == j, whole[:, :BE], 0.0), axis=1, keepdims=True)
        pivot = jnp.sum(jnp.where(sub == j, column, 0.0), axis=0, keepdims=True)
        root = lax.rsqrt(pivot)
        root = root * (1.5 - 0.5 * pivot * root * root)
        by = jnp.where(sub > j, column * (root * root), jnp.where(sub == j, 1.0 - root, 0.0))
        work[...] = whole - by * row
        return carry

    lax.fori_loop(0, BE, eliminate, 0)


def invert_step(k, schur, inverse, work):
    rows = slice(k * BE, (k + 1) * BE)
    rest = slice((k + 1) * BE, WIDE)
    work[:, :BE] = schur[rows, rows]
    work[:, BE:] = jnp.where(
        lax.broadcasted_iota(jnp.int32, (BE, BE), 0)
        == lax.broadcasted_iota(jnp.int32, (BE, BE), 1),
        1.0,
        0.0,
    ).astype(F32)
    factor_block(work)
    small = work[:, BE:]
    mine = highest(small, inverse[rows, :])
    inverse[rows, :] = mine
    if k + 1 < PANEL_BLOCKS:
        below = highest(schur[rest, rows], small, NT)
        schur[rest, rest] = schur[rest, rest] - highest(below, below, NT)
        inverse[rest, :] = inverse[rest, :] - highest(below, mine)


MESH = pl.DeviceIdType.MESH
PANEL_BLOCKS = WIDE // BE


def remote(source, target, send, recv, device):
    return pltpu.make_async_remote_copy(
        src_ref=source, dst_ref=target, send_sem=send, recv_sem=recv,
        device_id=device, device_id_type=MESH,
    )


class Exchange:
    def __init__(self, g, at, p, src, relay, dst, sems):
        self.g, self.p, self.src, self.relay, self.dst = g, p, src, relay, dst
        self.half, self.r, self.s = at
        (self.send, self.recv, self.relay_send, self.relay_recv, self.local) = sems

    def source(self, kind, x, y):
        return self.src.at[y, x, self.p] if kind else self.src.at[x, y, :, self.p]

    def peer(self, k):
        return (self.r + k // self.g) % self.g, (self.s + k % self.g) % self.g

    def turns(self, x, y):
        return jnp.logical_and(x != self.r, y // 2 != self.s // 2)

    def wanted(self, kind, a, b, x, y):
        if kind:
            return jnp.logical_not(use_direct(b, a, x, y))
        return use_direct(a, b, x, y)

    def first_hop(self, kind, k, x, y):
        g, r, s = self.g, self.r, self.s
        return remote(
            self.source(kind, x, y), self.relay.at[s, x, kind],
            self.send.at[kind * g * g + k], self.relay_recv.at[(s * g + x) * 2 + kind],
            (self.half, r, y),
        )

    def second_hop(self, kind, b, x):
        g, r, s = self.g, self.r, self.s
        target, slot = (
            (self.dst.at[b, r], b * g + r) if kind else (self.dst.at[r, b], r * g + b)
        )
        return remote(
            self.relay.at[b, x, kind], target,
            self.relay_send.at[(b * g + x) * 2 + kind], self.recv.at[slot],
            (self.half, x, s),
        )

    def whole_way(self, kind, k, x, y):
        g, r, s = self.g, self.r, self.s
        target, slot = (
            (self.dst.at[s, r], s * g + r) if kind else (self.dst.at[r, s], r * g + s)
        )
        return remote(
            self.source(kind, x, y), target,
            self.send.at[kind * g * g + k], self.recv.at[slot],
            (self.half, x, y),
        )

    def own(self):
        return pltpu.make_async_copy(
            self.source(0, self.r, self.s), self.dst.at[self.r, self.s], self.local.at[0]
        )

    def own_swap(self):
        return pltpu.make_async_copy(
            self.source(1, self.r, self.s), self.dst.at[self.s, self.r], self.local.at[1]
        )

    def start(self):
        g, r, s = self.g, self.r, self.s
        self.own().start()

        @pl.when(r != s)
        def _():
            self.own_swap().start()

        def turning(k, carry):
            x, y = self.peer(k)
            for kind in range(2):

                @pl.when(jnp.logical_and(self.turns(x, y), self.wanted(kind, r, s, x, y)))
                def _():
                    self.first_hop(kind, k, x, y).start()

            return carry

        lax.fori_loop(1, g * g, turning, 0)

        def straight(k, carry):
            x, y = self.peer(k)
            for kind in range(2):

                @pl.when(
                    jnp.logical_and(
                        jnp.logical_not(self.turns(x, y)), self.wanted(kind, r, s, x, y)
                    )
                )
                def _():
                    self.whole_way(kind, k, x, y).start()

            return carry

        lax.fori_loop(1, g * g, straight, 0)

    def for_relayed(self, act):
        g, r, s = self.g, self.r, self.s

        def one(k, carry):
            x = (r + k // g) % g
            b = (s + g - k % g) % g
            for kind in range(2):

                @pl.when(
                    jnp.logical_and(
                        jnp.logical_and(x != r, b // 2 != s // 2),
                        self.wanted(kind, r, b, x, s),
                    )
                )
                def _():
                    act(kind, b, x)

            return carry

        lax.fori_loop(1, g * g, one, 0)

    def pass_on(self):
        g = self.g

        def act(kind, b, x):
            remote(
                self.source(0, x, b), self.relay.at[b, x, kind],
                self.send.at[0], self.relay_recv.at[(b * g + x) * 2 + kind],
                (self.half, self.r, (self.s + 1) % g),
            ).wait_recv()
            self.second_hop(kind, b, x).start()

        self.for_relayed(act)

    def arrive(self):
        g, r, s = self.g, self.r, self.s

        def arrived(k, carry):
            a, b = k // g, k % g
            mine = jnp.logical_or(
                jnp.logical_and(a == r, b == s), jnp.logical_and(a == s, b == r)
            )

            @pl.when(jnp.logical_not(mine))
            def _():
                remote(
                    self.source(0, a, b), self.dst.at[a, b],
                    self.send.at[0], self.recv.at[k],
                    (self.half, (r + 1) % g, s),
                ).wait_recv()

            return carry

        lax.fori_loop(0, g * g, arrived, 0)
        self.own().wait()

        @pl.when(r != s)
        def _():
            self.own_swap().wait()

    def finish(self):
        g, r, s = self.g, self.r, self.s
        self.for_relayed(lambda kind, b, x: self.second_hop(kind, b, x).wait_send())

        def sent(k, carry):
            x, y = self.peer(k)
            for kind in range(2):

                @pl.when(self.wanted(kind, r, s, x, y))
                def _():
                    self.whole_way(kind, k, x, y).wait_send()

            return carry

        lax.fori_loop(1, g * g, sent, 0)


def exchange_sems(g):
    n = g * g
    return [
        pltpu.SemaphoreType.DMA((2 * n,)),
        pltpu.SemaphoreType.DMA((n,)),
        pltpu.SemaphoreType.DMA((2 * n,)),
        pltpu.SemaphoreType.DMA((2 * n,)),
        pltpu.SemaphoreType.DMA((2,)),
    ]


def position():
    return lax.axis_index("half"), lax.axis_index("row"), lax.axis_index("col")


def greet_half(g, at, barrier):
    half, r, s = at

    def greet(k, carry):
        pl.semaphore_signal(
            barrier, inc=1, device_id=(half, (r + k // g) % g, (s + k % g) % g),
            device_id_type=MESH,
        )
        return carry

    lax.fori_loop(1, g * g, greet, 0)


def spread_kernel(
    g, cap, slots, pick, where_at, has, turned, src, front, row_perm, col_perm,
    recv, relay, incoming, slab, near, far, out, lower_col,
    whole, stage, give, held, panel, strip, diagonal, inverse, schur, work, side, col_high, col_low, tiles, done, shown,
    sems, copy_sem,
    y_send, y_recv, slab_send, slab_recv, near_send, near_recv,
    far_send, far_recv, strip_send, strip_recv, diag_send, diag_recv, local, tile_sem, done_sem, shown_sem,
    give_send, give_recv, panel_sem,
):
    at = position()
    half, r, s = at
    other = (1 - half, r, s)
    group = half * g + r
    barrier = pltpu.get_barrier_semaphore()
    greet_half(g, at, barrier)

    def greet_other(k, carry):
        pl.semaphore_signal(
            barrier, inc=1, device_id=(1 - half, (r + k) % g, s), device_id_type=MESH
        )
        return carry

    lax.fori_loop(0, g, greet_other, 0)
    pl.semaphore_wait(barrier, g * g - 1 + g)

    pieces = [
        Exchange(g, at, q, src, relay.at[q], recv.at[q], sems[q]) for q in range(slots)
    ]
    pieces[0].start()
    panel_load = pltpu.make_async_copy(front.at[:, pl.ds(0, BE)], panel, panel_sem)
    panel_load.start()

    def over(j):
        return remote(stage.at[j], incoming.at[j], y_send.at[j], y_recv.at[j], other)

    def each(first_k, last_k, act):
        def one(k, carry):
            act(k)
            return carry

        lax.fori_loop(first_k, last_k, one, 0)

    def take(j):
        load = pltpu.make_async_copy(recv.at[j], whole, copy_sem)
        load.start()
        load.wait()

    def choose(j):
        def one(k):
            for a in range(cap):
                stage[j, a, k // slots, k % slots] = whole[pick[cap + a], k // slots, k % slots]

        each(0, g * slots, one)

    pieces[0].pass_on()
    pieces[0].arrive()
    for piece in pieces[1:2]:
        piece.start()
    take(0)
    lead = pick[2 * cap] // slots

    def choose_panel(i):
        for a in range(cap):
            give[a * slots + i] = whole[pick[cap + a], lead, i]

    each(0, slots, choose_panel)
    give_copy = remote(give, held.at[1], give_send, give_recv, other)
    give_copy.start()

    def hold_panel(i):
        for a in range(cap):
            held[0, a * slots + i] = whole[pick[a], lead, i]

    each(0, slots, hold_panel)
    if slots > 1:
        choose(0)
    panel_load.wait()
    give_copy.wait()
    if slots > 1:
        over(0).start()

    def add_panel(t):
        rows = pl.ds(pl.multiple_of(t * BE, BE), BE)
        total = panel[rows, :]
        for c in range(2):
            at = where_at[c, t]
            block = held[c, at]
            lying = jnp.full((BE, BE), turned[c, t], jnp.int32) == 1
            block = jnp.where(lying, block.T, block)
            moved = highest(
                highest(row_perm[c, at].astype(F32), block),
                col_perm[c, pick[2 * cap + c]].astype(F32), NT,
            )
            total += jnp.where(jnp.full((BE, BE), has[c, t], jnp.int32) == 1, moved, 0.0)
        panel[rows, :] = total

    each(0, panel.shape[0] // BE, add_panel)

    holds = s < PANEL_BLOCKS
    at_col = jnp.minimum(s, PANEL_BLOCKS - 1)
    own_slab = pltpu.make_async_copy(panel, slab.at[at_col], local.at[0])
    own_near = pltpu.make_async_copy(panel, near.at[at_col], local.at[1])

    def slab_copy(k):
        return remote(
            panel, slab.at[at_col], slab_send.at[k], slab_recv.at[at_col],
            (half, r, (s + k) % g),
        )

    def near_copy(k):
        return remote(
            panel, near.at[at_col], near_send.at[k], near_recv.at[at_col],
            (half, (r + k) % g, r),
        )

    gives = jnp.logical_and(holds, jnp.logical_and(half == 0, r < PANEL_BLOCKS))
    at_row = jnp.minimum(r, PANEL_BLOCKS - 1)
    top = panel.at[pl.ds(0, BE)]
    own_strip = pltpu.make_async_copy(top, strip.at[at_row], local.at[2])
    own_diag = pltpu.make_async_copy(strip, diagonal.at[at_col], local.at[3])

    def strip_copy(k):
        to = (group + k) % (2 * g)
        return remote(
            top, strip.at[at_row], strip_send.at[k], strip_recv.at[at_row],
            (to // g, to % g, s),
        )

    def diag_copy(k):
        return remote(
            strip, diagonal.at[at_col], diag_send.at[k], diag_recv.at[at_col],
            (half, r, (s + k) % g),
        )

    @pl.when(gives)
    def _():
        own_strip.start()
        each(1, 2 * g, lambda k: strip_copy(k).start())

    def strip_in(q):
        @pl.when(jnp.logical_not(jnp.logical_and(half == 0, r == q)))
        def _():
            remote(
                top, strip.at[q], strip_send.at[0], strip_recv.at[q], other
            ).wait_recv()

    @pl.when(holds)
    def _():
        each(0, PANEL_BLOCKS, strip_in)

        @pl.when(gives)
        def _():
            own_strip.wait()

        own_diag.start()
        each(1, g, lambda k: diag_copy(k).start())
        own_slab.start()
        each(1, g, lambda k: slab_copy(k).start())

        @pl.when(s == r)
        def _():
            own_near.start()

        def near_start(k):
            @pl.when(jnp.logical_or(k != 0, s != r))
            def _():
                near_copy(k).start()

        each(0, g, near_start)

    def hand_over(j):
        take(j)
        choose(j)
        over(j).start()

    if slots > 1:
        pieces[1].pass_on()

    def diag_in(q):
        @pl.when(q != s)
        def _():
            remote(
                strip, diagonal.at[q], diag_send.at[0], diag_recv.at[q], (half, r, (s + 1) % g)
            ).wait_recv()

    each(0, PANEL_BLOCKS, diag_in)

    @pl.when(holds)
    def _():
        own_diag.wait()

    for a in range(PANEL_BLOCKS):
        for b in range(PANEL_BLOCKS):
            schur[a * BE : (a + 1) * BE, b * BE : (b + 1) * BE] = diagonal[b, a]
    eye = jnp.where(
        lax.broadcasted_iota(jnp.int32, (WIDE, WIDE), 0)
        == lax.broadcasted_iota(jnp.int32, (WIDE, WIDE), 1),
        1.0,
        0.0,
    ).astype(F32)
    inverse[...] = eye
    far_copy = remote(near, far, far_send, far_recv, other)

    def near_in(q):
        @pl.when(jnp.logical_not(jnp.logical_and(r == s, q == s)))
        def _():
            remote(
                panel, near.at[q], near_send.at[0], near_recv.at[q], (half, r, (s + 1) % g)
            ).wait_recv()

    def nears_in():
        each(0, PANEL_BLOCKS, near_in)

        @pl.when(jnp.logical_and(holds, s == r))
        def _():
            own_near.wait()

        far_copy.start()

    def slab_in(q):
        @pl.when(q != s)
        def _():
            remote(
                panel, slab.at[q], slab_send.at[0], slab_recv.at[q], (half, r, (s + 1) % g)
            ).wait_recv()

    def fetch(array):
        load = pltpu.make_async_copy(array, side, copy_sem)
        load.start()
        load.wait()

    tall = tiles.shape[1]
    count = front.shape[0] // tall

    def lower(t):
        rows = pl.ds(pl.multiple_of(t * tall, tall), tall)
        return highest(
            jnp.concatenate([side[q, rows, :] for q in range(PANEL_BLOCKS)], axis=1),
            inverse[...], NT,
        )

    def column_side(array, h):
        fetch(array)

        def one(t):
            high, low = split(lower(t))
            for k in range(tall // BE):
                at = pl.ds(pl.multiple_of((2 * (t * (tall // BE) + k) + h) * BE, BE), BE)
                col_high[at, :] = high[k * BE : (k + 1) * BE]
                col_low[at, :] = low[k * BE : (k + 1) * BE]

        each(0, count, one)

    def tile_load(t):
        rows = pl.ds(pl.multiple_of(t * tall, tall), tall)
        return pltpu.make_async_copy(front.at[rows], tiles.at[t % 2], tile_sem.at[t % 2])

    def tile_store(t):
        rows = pl.ds(pl.multiple_of(t * tall, tall), tall)
        return pltpu.make_async_copy(done.at[t % 2], out.at[rows], done_sem.at[t % 2])

    def tile(t):
        @pl.when(t + 1 < count)
        def _():
            tile_load(t + 1).start()

        tile_load(t).wait()

        @pl.when(t >= 2)
        def _():
            tile_store(t - 2).wait()

        rows = lower(t)
        mine = rows[:, :BE]
        for q in range(1, PANEL_BLOCKS):
            mine = jnp.where(s == q, rows[:, q * BE : (q + 1) * BE], mine)
        hidden = jnp.logical_and(
            jnp.logical_and(t == 0, group < PANEL // BE), s >= PANEL // BE
        )
        line = lax.broadcasted_iota(jnp.int32, mine.shape, 0)
        shown[pl.ds(pl.multiple_of(t * tall, tall), tall), :] = jnp.where(
            jnp.logical_and(hidden, line < BE), 0.0, mine
        )
        high, low = split(rows)
        width = out.shape[1]
        wide = WIDE if width % WIDE == 0 else 2 * BE
        slot = t % 2
        for at in range(0, width, wide):
            cols = slice(at, at + wide)
            ch = col_high[cols, :]
            total = lax.dot_general(high, ch, NT, preferred_element_type=F32)
            total += lax.dot_general(low, ch, NT, preferred_element_type=F32)
            total += lax.dot_general(high, col_low[cols, :], NT, preferred_element_type=F32)
            done[slot, :, cols] = tiles[slot, :, cols] - total
        tile_store(t).start()

    def advance(k):
        if 0 < k < slots - 1:
            pieces[k].arrive()
            hand_over(k)
            pieces[k + 1].pass_on()

    invert_step(0, schur, inverse, work)
    nears_in()
    for piece in pieces[2:3]:
        piece.start()
    invert_step(1, schur, inverse, work)
    for piece in pieces[3:]:
        piece.start()
    advance(1)
    invert_step(2, schur, inverse, work)
    invert_step(3, schur, inverse, work)
    column_side(near, half)
    far_copy.wait()
    column_side(far, 1 - half)
    advance(2)
    each(0, PANEL_BLOCKS, slab_in)

    @pl.when(holds)
    def _():
        own_slab.wait()

    fetch(slab)
    tile_load(0).start()
    each(0, count, tile)
    for k in range(3, slots):
        advance(k)
    tile_store(count - 2).wait()
    tile_store(count - 1).wait()
    shown_store = pltpu.make_async_copy(shown, lower_col, shown_sem)
    shown_store.start()
    if slots > 1:
        pieces[-1].arrive()
    for piece in pieces:
        piece.finish()
    for j in range(slots - 1):
        over(j).wait()
    shown_store.wait()

    @pl.when(holds)
    def _():
        each(1, g, lambda k: slab_copy(k).wait_send())
        each(1, g, lambda k: diag_copy(k).wait_send())

        def near_out(k):
            @pl.when(jnp.logical_or(k != 0, s != r))
            def _():
                near_copy(k).wait_send()

        each(0, g, near_out)

    @pl.when(gives)
    def _():
        each(1, 2 * g, lambda k: strip_copy(k).wait_send())


def spread(packed, front, t, g, cap):
    slots = packed.shape[2]
    later = max(slots - 1, 1)
    blocks = (slots, BE, BE)
    rows, cols = front.shape
    slab = (PANEL_BLOCKS, rows, BE)
    tall = 2 * BE if rows % (2 * BE) == 0 else BE
    dma = pltpu.SemaphoreType.DMA
    return pl.pallas_call(
        functools.partial(spread_kernel, g, cap, slots),
        out_shape=[
            jax.ShapeDtypeStruct((slots, g, g) + blocks, F32),
            jax.ShapeDtypeStruct((slots, g, g, 2) + blocks, F32),
            jax.ShapeDtypeStruct((later, cap, g) + blocks, F32),
            jax.ShapeDtypeStruct(slab, F32),
            jax.ShapeDtypeStruct(slab, F32),
            jax.ShapeDtypeStruct(slab, F32),
            jax.ShapeDtypeStruct(front.shape, F32),
            jax.ShapeDtypeStruct((rows, BE), F32),
        ],
        in_specs=[pl.BlockSpec(memory_space=pltpu.SMEM)] * 4
        + [pl.BlockSpec(memory_space=pl.ANY)] * 2
        + [pl.BlockSpec(memory_space=pltpu.VMEM)] * 2,
        out_specs=[pl.BlockSpec(memory_space=pl.ANY)] * 8,
        scratch_shapes=[
            pltpu.VMEM((g, g) + blocks, F32),
            pltpu.VMEM((later, cap, g) + blocks, F32),
            pltpu.VMEM((cap * slots, BE, BE), F32),
            pltpu.VMEM((2, cap * slots, BE, BE), F32),
            pltpu.VMEM((rows, BE), F32),
            pltpu.VMEM((PANEL_BLOCKS, BE, BE), F32),
            pltpu.VMEM((PANEL_BLOCKS, PANEL_BLOCKS, BE, BE), F32),
            pltpu.VMEM((WIDE, WIDE), F32),
            pltpu.VMEM((WIDE, WIDE), F32),
            pltpu.VMEM((BE, 2 * BE), F32),
            pltpu.VMEM(slab, F32),
            pltpu.VMEM((cols, WIDE), BF16),
            pltpu.VMEM((cols, WIDE), BF16),
            pltpu.VMEM((2, tall, cols), F32),
            pltpu.VMEM((2, tall, cols), F32),
            pltpu.VMEM((rows, BE), F32),
            [exchange_sems(g) for _ in range(slots)],
            dma,
            dma((later,)),
            dma((later,)),
            dma((g,)),
            dma((PANEL_BLOCKS,)),
            dma((g,)),
            dma((PANEL_BLOCKS,)),
            dma,
            dma,
            dma((2 * g,)),
            dma((PANEL_BLOCKS,)),
            dma((g,)),
            dma((PANEL_BLOCKS,)),
            dma((4,)),
            dma((2,)),
            dma((2,)),
            dma,
            dma,
            dma,
            dma,
        ],
        compiler_params=pltpu.CompilerParams(
            collective_id=0, has_side_effects=True, vmem_limit_bytes=60 * 1024 * 1024
        ),
    )(
        t["pick"], t["where_at"], t["has"], t["turned"], packed, front, t["row_perm"], t["col_perm"]
    )


def split(x):
    high = x.astype(BF16)
    return high, (x - high.astype(F32)).astype(BF16)


def place_kernel(
    g, slots, cap, sets, finish, refs_at, child_of, piece_of, a_of, blocks_at,
    t_at, u_at, swapped, valid, place_of, *refs,
):
    front = refs[0]
    chunks = refs[1 : 1 + sets]
    row_perm, col_perm, lower_col, out, acc, mid, sem = refs[1 + sets :]
    n = pl.program_id(0)
    c, p, a = child_of[n], piece_of[n], a_of[n]
    ca = c * cap + a

    @pl.when(n == 0)
    def _():
        load = pltpu.make_async_copy(front, acc, sem)
        load.start()
        load.wait()

    def body(chunk):
        for s in range(g):
            turned = swapped[ca * g + s]

            def moved_rows(i, x):
                high, low = split(x)
                perm = row_perm[c, a * slots + i]
                rows = slice(i * BE, (i + 1) * BE)
                mid[s, rows, :] = jnp.dot(
                    perm, jnp.concatenate([high, low], axis=1), preferred_element_type=F32
                ).astype(BF16)

            lying = jnp.full((BE, BE), turned, jnp.int32) == 1
            for i in range(slots):
                block = chunk[0, s, i]
                moved_rows(i, jnp.where(lying, block.T, block))

            perm = col_perm[c, s * slots + p]
            moved = lax.dot_general(
                mid[s], jnp.concatenate([perm, perm], axis=1), NT, preferred_element_type=F32
            )
            u = pl.multiple_of(u_at[(c * g + s) * slots + p] * BE, BE)
            for i in range(slots):
                t = pl.multiple_of(t_at[ca * slots + i] * BE, BE)
                acc[pl.ds(t, BE), pl.ds(u, BE)] += moved[i * BE : (i + 1) * BE]

    for m in range(sets):
        @pl.when(jnp.logical_and(refs_at[n] == m, valid[ca] == 1))
        def _():
            body(chunks[m])

    @pl.when(n == pl.num_programs(0) - 1)
    def _():
        if finish:
            @pl.when(place_of[0] < PANEL_BLOCKS)
            def _():
                acc[:BE, :] = jnp.zeros((BE, acc.shape[1]), F32)

            @pl.when(place_of[1] < PANEL_BLOCKS)
            def _():
                acc[:, :BE] = lower_col[...]

        store = pltpu.make_async_copy(acc, out, sem)
        store.start()
        store.wait()


def place(front, sets, steps, mine, t, place_of, lower_col, g, slots, cap, finish):
    held = []
    for m in range(len(sets)):
        now = next(step[1] for step in steps if step[0] == m)
        for step in steps:
            now = step[1] if step[0] == m else now
            held.append(now)
    count = len(steps)
    ints = lambda k: np.asarray([step[k] for step in steps], np.int32)
    base = np.asarray([offset for offset, a in held], np.int32)
    hot = np.asarray([[a == b for b in range(cap)] for offset, a in held], np.int32)
    at = base + jnp.sum(hot * mine, axis=1)
    chunk = lambda m: pl.BlockSpec(
        (1, g, slots, BE, BE), lambda n, *refs: (refs[4][m * count + n], 0, 0, 0, 0)
    )
    perms = lambda x: pl.BlockSpec(x.shape, lambda n, *_: (0, 0, 0, 0))
    return pl.pallas_call(
        functools.partial(place_kernel, g, slots, cap, len(sets), finish),
        grid_spec=pltpu.PrefetchScalarGridSpec(
            num_scalar_prefetch=10,
            grid=(count,),
            in_specs=[pl.BlockSpec(memory_space=pl.ANY)]
            + [chunk(m) for m in range(len(sets))]
            + [
                perms(t["row_perm"]),
                perms(t["col_perm"]),
                pl.BlockSpec((front.shape[0], BE), lambda n, *_: (0, 0)),
            ],
            out_specs=pl.BlockSpec(memory_space=pl.ANY),
            scratch_shapes=[
                pltpu.VMEM(front.shape, F32),
                pltpu.VMEM((g, slots * BE, 2 * BE), BF16),
                pltpu.SemaphoreType.DMA,
            ],
        ),
        out_shape=jax.ShapeDtypeStruct(front.shape, F32),
        compiler_params=pltpu.CompilerParams(vmem_limit_bytes=60 * 1024 * 1024),
        cost_estimate=pl.CostEstimate(
            flops=4_000_000_000, bytes_accessed=36_000_000, transcendentals=0
        ),
    )(
        ints(0), ints(2), ints(3), ints(4), at,
        t["t_at"], t["u_at"], t["swapped"], t["valid"], place_of,
        front, *sets, t["row_perm"], t["col_perm"], lower_col,
    )


def pick(hits, count):
    ids = jnp.arange(hits.shape[-1])
    earlier = jnp.logical_and(hits[..., None, :], ids[None, :] < ids[:, None])
    rank = jnp.sum(earlier.astype(jnp.int32), axis=-1)
    chosen = jnp.logical_and(hits[..., None, :], rank[..., None, :] == jnp.arange(count)[:, None])
    return chosen, jnp.sum(jnp.where(chosen, ids, 0), axis=-1)


def all_tables(
    child_map, grid_size, group_count, my_row, my_col, my_half, cap, slots, row_blocks_count
):
    g, n = grid_size, slots
    halves = child_map.shape[0]
    maps = child_map.reshape(halves, n * g, g, BE).transpose(0, 2, 1, 3)
    block = maps[..., 0] // BE
    inner = maps % BE
    target = block % g
    before = jnp.logical_and(
        target[..., None, :] == target[..., :, None], block[..., None, :] < block[..., :, None]
    )
    at = target * n + jnp.sum(before.astype(jnp.int32), axis=-1)
    hot = at[..., None, :] == jnp.arange(n * g)[:, None]
    order = jnp.sum(jnp.where(hot, jnp.arange(n * g), 0), axis=-1)
    blocks = jnp.sum(jnp.where(hot, block[..., None, :], 0), axis=-1)

    def of_target(x, which):
        return lax.dynamic_slice_in_dim(x, which * n, n, axis=2)

    inner_of = jnp.sum(
        jnp.where(hot[..., None], inner[:, :, None], 0), axis=3
    )
    row_blocks = of_target(blocks, my_row)
    col_blocks = of_target(blocks, my_col)
    half_of = row_blocks[..., 0] % group_count // g
    hit = half_of == my_half
    chosen, mine = pick(hit, cap)
    _, other = pick(jnp.logical_not(hit), cap)
    valid = jnp.any(chosen, axis=-1)
    mine_rows = jnp.sum(jnp.where(chosen[..., None], row_blocks[:, None], 0), axis=2)
    row_inner = jnp.sum(
        jnp.where(chosen[..., None, None], of_target(inner_of, my_row)[:, None], 0), axis=2
    )
    lanes = jnp.arange(BE)[:, None]
    residues = jnp.arange(g)
    swapped = jnp.logical_not(use_direct(mine[..., None], residues, my_row, my_col))
    lead = col_blocks[..., 0] < g
    lead_at = jnp.sum(jnp.where(lead, residues, 0), axis=-1)
    fits = jnp.logical_and(
        (mine_rows // group_count)[..., None] == jnp.arange(row_blocks_count),
        jnp.logical_and(valid, jnp.any(lead, axis=-1)[:, None])[..., None, None],
    )
    block_id = (jnp.arange(cap)[:, None] * n + jnp.arange(n))[..., None]
    across = jnp.logical_not(use_direct(mine, lead_at[:, None], my_row, my_col))
    tables = {
        "order": order,
        "picks": jnp.concatenate([mine, other], axis=1),
        "leads": lead_at * n,
        "where_at": jnp.sum(jnp.where(fits, block_id, 0), axis=(1, 2)),
        "has": jnp.sum(fits.astype(jnp.int32), axis=(1, 2)),
        "turned": jnp.sum(
            jnp.logical_and(fits, across[..., None, None]).astype(jnp.int32), axis=(1, 2)
        ),
        "valid": valid.astype(jnp.int32),
        "swapped": swapped.astype(jnp.int32).reshape(halves, -1),
        "t_at": (mine_rows // group_count).reshape(halves, -1),
        "u_at": (col_blocks // g).reshape(halves, -1),
        "row_perm": (row_inner[..., None, :] == lanes).astype(BF16).reshape(halves, -1, BE, BE),
        "col_perm": (of_target(inner_of, my_col)[..., None, :] == lanes)
        .astype(BF16).reshape(halves, -1, BE, BE),
    }

    flat = ("valid", "swapped", "t_at", "u_at")

    def own_first(k, v):
        v = jnp.where(my_half == 0, v, v[::-1])
        return v.reshape(-1) if k in flat else v

    t = {k: own_first(k, v) for k, v in tables.items()}
    t["pick"] = jnp.concatenate([t["picks"][0], t["leads"]])
    return t


def on_device(front_init, child_update, child_map):
    grid_size = lax.axis_size("row")
    halves = lax.axis_size("half")
    group_count = halves * grid_size
    my_half = lax.axis_index("half")
    my_row = lax.axis_index("row")
    my_col = lax.axis_index("col")
    my_group = my_half * grid_size + my_row
    slots = child_update.shape[1] // BE // grid_size
    front_rows, front_cols = front_init.shape
    row_blocks = front_rows // BE
    cap = min(grid_size, row_blocks // slots)
    t = all_tables(
        child_map, grid_size, group_count, my_row, my_col, my_half, cap, slots, row_blocks
    )
    orders = t["order"][0]
    pick = t["pick"]
    packed = pack(
        child_update[0],
        lax.dynamic_index_in_dim(orders, my_row, 0, keepdims=False),
        lax.dynamic_index_in_dim(orders, my_col, 0, keepdims=False),
        grid_size,
        slots,
    )
    recv, _, incoming, _, _, _, front, lower_col = spread(packed, front_init, t, grid_size, cap)
    blocks = (grid_size, slots, BE, BE)

    def chosen(a):
        return lax.dynamic_slice(
            recv, (slots - 1, pick[cap + a], 0, 0, 0, 0), (1, 1) + blocks
        )[0]

    outgoing = jnp.concatenate([chosen(a) for a in range(cap)], axis=0)
    final = lax.ppermute(outgoing, "half", [(0, 1), (1, 0)])
    place_of = jnp.stack([my_group, my_col]).astype(jnp.int32)
    mine = pick[:cap]
    sets = [recv.reshape((-1,) + blocks), incoming.reshape((-1,) + blocks)]
    steps = []
    for p in range(slots):
        steps += [(0, (p * grid_size, a), 0, p, a) for a in range(cap)]
    for p in range(slots - 1):
        steps += [(1, (p * cap + a, -1), 1, p, a) for a in range(cap)]
    if slots == 1:
        sets = sets[:1]
    front = place(
        front, sets, steps, mine, t, place_of, lower_col, grid_size, slots, cap, False
    )
    steps = [(0, (a, -1), 1, slots - 1, a) for a in range(cap)]
    return place(
        front, [final], steps, mine, t, place_of, lower_col, grid_size, slots, cap, True
    )


def solution(mesh):
    placed = (P(("half", "row"), "col"), P("half", "row", "col"), P())
    return jax.shard_map(
        on_device, mesh=mesh, in_specs=placed, out_specs=P(("half", "row"), "col"), check_vma=False
    )
```
